32 devices in a mesh: pix: 16 (over z, x, core), rep: 2 (over y).
Axes of the slice: x: 2, y: 2, z: 4, core: 2. Of those that a mesh axis runs over, the one named last changes fastest.
Arguments:
- tokens: bfloat16 [256, 16, 1152], P(('pix', 'rep')), may hold values from -48 to 48
- out_grad: bfloat16 [256, 16, 1152], P(('pix', 'rep')), may hold values from -6 to 6
- query_weight: bfloat16 [1152, 1152], P('pix'), may hold values from -0.1875 to 0.1875
- key_weight: bfloat16 [1152, 1152], P('pix'), may hold values from -0.1875 to 0.1875
- value_weight: bfloat16 [1152, 1152], P('pix'), may hold values from -0.1875 to 0.1875
- output_weight: bfloat16 [1152, 1152], P('pix'), may hold values from -0.1875 to 0.1875
Outputs:
- input_grad: bfloat16 [256, 16, 1152], P(('pix', 'rep'))
- weight_grads: float32 [1152, 4608], P('pix')
The draws below stay inside these ranges and needn't reach their ends.
All inputs are finite; a program needn't handle non-finite values.
Results may differ from the reference program's by a relative error of at most 0.025.
The reference program's roundings to bfloat16 on the way count: a program that leaves them out, or rounds other values in their place, can miss the bound.
Values may be sent and summed in bfloat16 or wider, within the bound.
No kernel may reach another device: no remote copies, remote signals or barrier semaphores. Data moves between devices by JAX's collectives and lax.ppermute only.
A program may use at most 128 MiB of HBM per device.

```python
import jax
import jax.numpy as jnp
from jax import lax

D = 1152
HEADS = 16
HEAD_DIM = 72
FRAMES = 16
SITE_DEV = 8
SITES = 256
N_PIX = 16
N_REP = 2


def draw_tokens(key, part):
    base_key, perm_key = jax.random.split(jax.random.fold_in(key, 11), 2)
    base = jnp.clip(jax.random.normal(base_key, (SITES, FRAMES, D), jnp.float32), -4.0, 4.0)
    sites = jnp.arange(SITES, dtype=jnp.int32)
    pix_index = sites // SITE_DEV // N_REP
    paired = jax.random.permutation(perm_key, N_PIX)
    column_block = jnp.arange(D, dtype=jnp.int32) // (D // N_PIX)
    chosen = paired[pix_index]
    spike = jnp.where(column_block[None, :] == chosen[:, None], 3.0, 1.0)
    values = base * spike[:, None, :]
    return values.astype(jnp.bfloat16)


def block_scale(stream_key, extent, shards, least, high):
    def one(position, parts):
        heights = jax.random.uniform(jax.random.fold_in(jax.random.fold_in(stream_key, 6), position), (parts,), jnp.float32, least / len(shards), high / len(shards))
        return jnp.repeat(jnp.exp(heights), extent[position] // parts).reshape((-1,) + (1,) * (len(extent) - position - 1))

    level = one(*shards[0])
    for cut in shards[1:]:
        level = level * one(*cut)
    return level


def noise(stream_key, shape, deviation, limit, cuts=(), held_as=jnp.bfloat16):
    values = jax.random.normal(stream_key, shape, jnp.float32) * deviation
    if len(cuts) > 0:
        values = block_scale(stream_key, shape, cuts, -0.22, 0.18) * values
    return jnp.clip(values, min=-limit, max=limit).astype(held_as)


def setup_inputs(seed: int = 0) -> dict:
    key_of = jax.random.split(jax.random.key(seed), 7)
    return {
        "tokens": draw_tokens(jax.random.fold_in(key_of[6], 71), 0),
        "out_grad": noise(key_of[1], (SITES, FRAMES, D), 1.0, 6.0, ((0, 32),)),
        "query_weight": noise(key_of[2], (D, D), D ** -0.5, 0.1875, ((0, 16),)),
        "key_weight": noise(key_of[3], (D, D), D ** -0.5, 0.1875, ((0, 16),)),
        "value_weight": noise(key_of[4], (D, D), D ** -0.5, 0.1875, ((0, 16),)),
        "output_weight": noise(key_of[5], (D, D), D ** -0.5, 0.1875, ((0, 16),)),
    }


def contract_last(left, right):
    return lax.dot_general(left, right, (((1,), (1,)), ((), ())), preferred_element_type=jnp.float32)


def contract_first(left, right):
    return lax.dot_general(left, right, (((0,), (0,)), ((), ())), preferred_element_type=jnp.float32)


def block_step(block_x, block_d, query_weight, key_weight, value_weight, output_weight):
    count = block_x.shape[0]
    rows = block_x.reshape(-1, D)
    drows = block_d.reshape(-1, D)
    scale = 1.0 / (HEAD_DIM ** 0.5)
    query = jnp.dot(rows, query_weight, preferred_element_type=jnp.float32).astype(jnp.bfloat16)
    keyed = jnp.dot(rows, key_weight, preferred_element_type=jnp.float32).astype(jnp.bfloat16)
    valued = jnp.dot(rows, value_weight, preferred_element_type=jnp.float32).astype(jnp.bfloat16)
    shape4 = (count, FRAMES, HEADS, HEAD_DIM)
    qh = query.reshape(shape4).astype(jnp.float32)
    kh = keyed.reshape(shape4).astype(jnp.float32)
    vh = valued.reshape(shape4).astype(jnp.float32)
    scores = jnp.einsum('sfhe,sghe->shfg', qh, kh) * scale
    scores = scores - jnp.max(scores, axis=-1, keepdims=True)
    expo = jnp.exp(scores)
    probs = expo / jnp.sum(expo, axis=-1, keepdims=True)
    probs_b = probs.astype(jnp.bfloat16).astype(jnp.float32)
    attended = jnp.einsum('shfg,sghe->sfhe', probs_b, vh).reshape(-1, D).astype(jnp.bfloat16)
    dattn = contract_last(drows, output_weight).astype(jnp.bfloat16)
    dah = dattn.reshape(shape4).astype(jnp.float32)
    dvalue = jnp.einsum('shfg,sfhe->sghe', probs_b, dah).reshape(-1, D).astype(jnp.bfloat16)
    dprobs = jnp.einsum('sfhe,sghe->shfg', dah, vh)
    dscore = (probs * (dprobs - jnp.sum(dprobs * probs, axis=-1, keepdims=True)) * scale).astype(jnp.bfloat16).astype(jnp.float32)
    dquery = jnp.einsum('shfg,sghe->sfhe', dscore, kh).reshape(-1, D).astype(jnp.bfloat16)
    dkey = jnp.einsum('shfg,sfhe->sghe', dscore, qh).reshape(-1, D).astype(jnp.bfloat16)
    dinput = contract_last(dquery, query_weight) + contract_last(dkey, key_weight) + contract_last(dvalue, value_weight)
    partial_value = jnp.concatenate([contract_first(rows, dquery), contract_first(rows, dkey), contract_first(rows, dvalue), contract_first(attended, drows)], axis=1)
    partial_value = lax.optimization_barrier(partial_value.astype(jnp.bfloat16)).astype(jnp.float32)
    return dinput.astype(jnp.bfloat16).reshape(count, FRAMES, D), partial_value


def reference(tokens, out_grad, query_weight, key_weight, value_weight, output_weight):
    blocks = tokens.shape[0] // SITE_DEV
    xs = tokens.reshape(blocks, SITE_DEV, FRAMES, D)
    ds = out_grad.reshape(blocks, SITE_DEV, FRAMES, D)

    def step(total, pair):
        dinput, partial_value = block_step(pair[0], pair[1], query_weight, key_weight, value_weight, output_weight)
        return total + partial_value, dinput

    init = jnp.zeros((D, 4 * D), jnp.float32)
    total, dinputs = lax.scan(step, init, (xs, ds))
    return dinputs.reshape(tokens.shape), total
```

```python
import jax
import jax.numpy as jnp
from jax import lax
from jax.sharding import PartitionSpec as P

HEADS = 16
FRAMES = 16
BOTH = ("pix", "rep")


def matmul(left, right, dims):
    return lax.dot_general(left, right, (dims, ((), ())), preferred_element_type=jnp.float32)


class Grid:
    def __init__(self, pix, rep):
        self.lines, self.groups, self.rep = pix // 4, rep // 2, rep

    def all(self):
        for a in range(self.lines):
            for b in range(2):
                for c in range(2):
                    for g in range(self.groups):
                        for y in range(2):
                            yield a, b, c, g, y

    def flat(self, a, b, c, g, y):
        return (4 * a + 2 * b + c) * self.rep + 2 * g + y

    def send(self, value, target):
        pairs = []
        for source in self.all():
            to = target(*source)
            if to is not None:
                pairs.append((self.flat(*source), self.flat(*to)))
        return lax.ppermute(value, BOTH, pairs)

    def flip(self, value, db, dc, dy):
        return self.send(value, lambda a, b, c, g, y: (a, b ^ db, c ^ dc, g, y ^ dy))

    def shift(self, value, step):
        return self.send(value, lambda a, b, c, g, y: ((a + step) % self.lines, b, c, g, y))


def pick(stacked, index):
    return lax.dynamic_index_in_dim(stacked, index, 0, keepdims=False)


def ordered(own, other, bit):
    return jnp.where(bit == 0, own, other), jnp.where(bit == 0, other, own)


def attention(query, keyed, valued, dattn, scale):
    scores = jnp.einsum("sfhe,sghe->shfg", query, keyed, preferred_element_type=jnp.float32) * scale
    scores = scores - jnp.max(scores, axis=-1, keepdims=True)
    expo = jnp.exp(scores)
    probs = expo / jnp.sum(expo, axis=-1, keepdims=True)
    probs_b = probs.astype(jnp.bfloat16)
    attended = jnp.einsum("shfg,sghe->sfhe", probs_b, valued, preferred_element_type=jnp.float32)
    dvalue = jnp.einsum("shfg,sfhe->sghe", probs_b, dattn, preferred_element_type=jnp.float32)
    dprobs = jnp.einsum("sfhe,sghe->shfg", dattn, valued, preferred_element_type=jnp.float32)
    dscore = (probs * (dprobs - jnp.sum(dprobs * probs, axis=-1, keepdims=True)) * scale).astype(
        jnp.bfloat16
    )
    dquery = jnp.einsum("shfg,sghe->sfhe", dscore, keyed, preferred_element_type=jnp.float32)
    dkey = jnp.einsum("shfg,sfhe->sghe", dscore, query, preferred_element_type=jnp.float32)
    return tuple(v.astype(jnp.bfloat16) for v in (attended, dquery, dkey, dvalue))


def local(pix, rep, tokens, out_grad, query_weight, key_weight, value_weight, output_weight):
    grid = Grid(pix, rep)
    lines = grid.lines
    width = tokens.shape[-1]
    dim = width // HEADS
    shard = query_weight.shape[0]
    scale = 1.0 / dim**0.5
    place, rank = lax.axis_index("pix"), lax.axis_index("rep")
    a, b, c, y = place // 4, (place // 2) % 2, place % 2, rank % 2
    rows = tokens.reshape(-1, width)
    drows = out_grad.reshape(-1, width)
    count = rows.shape[0]

    def gather_rows(own):
        chips = [own] + [grid.flip(own, db, 0, dy) for db, dy in ((1, 0), (0, 1), (1, 1))]
        return jnp.concatenate(chips + [grid.flip(one, 0, 1, 0) for one in chips], axis=0)

    weights = jnp.stack([query_weight, key_weight, value_weight], axis=1)
    weights = weights.reshape(shard, 3, HEADS // 8, 2, 2, 2, dim)
    kept = HEADS // 8
    mine = lax.dynamic_index_in_dim(
        weights.reshape(shard, 3, 2, kept, 2, 2, dim), y, 5, keepdims=False
    )
    mine = mine.transpose(4, 2, 0, 1, 3, 5).reshape(2, 2, shard, 3 * kept * dim)

    def piece(db, dc):
        return pick(pick(mine, b ^ db), c ^ dc)

    near = [piece(0, 0), grid.flip(piece(0, 1), 0, 1, 0)]
    far = [grid.flip(piece(1, 0), 1, 0, 0), grid.flip(piece(1, 1), 1, 1, 0)]
    near_rows = jnp.concatenate(ordered(near[0], near[1], c), axis=0)
    far_rows = jnp.concatenate(ordered(far[0], far[1], c), axis=0)
    plane = jnp.concatenate(ordered(near_rows, far_rows, b), axis=0)
    full_rows = gather_rows(rows)
    planes = jnp.stack([plane] + [grid.shift(plane, s) for s in range(1, lines)])
    full_w = jnp.concatenate([pick(planes, (a - at) % lines) for at in range(lines)], axis=0)

    one_head = shard == dim
    if one_head:
        span = lines // 2
        held = grid.send(
            output_weight, lambda a, b, c, g, y: (a, b, a // span, g, y) if c == y else None
        )
        heads = [held]
        for s in range(1, lines):
            heads.append(
                grid.send(
                    held,
                    lambda a, b, c, g, y: ((a + s) % lines, b, c, g, y) if a // span == c else None,
                )
            )
        heads = jnp.stack(heads)
        out_w = jnp.concatenate([pick(heads, (a - span * c - k) % lines) for k in range(kept)], axis=0)
    else:
        everything = lax.all_gather(output_weight, "pix", axis=0, tiled=True)
        everything = everything.reshape(2, kept, 2, 2, dim, width)
        out_w = lax.dynamic_index_in_dim(
            pick(everything, c).reshape(kept, 4, dim, width), 2 * b + y, 1, keepdims=False
        ).reshape(kept * dim, width)
    full_drows = gather_rows(drows)

    total = full_rows.shape[0]
    shape4 = (total // FRAMES, FRAMES, kept, dim)
    qkv = matmul(full_rows, full_w, ((1,), (0,))).astype(jnp.bfloat16)
    dattn = matmul(full_drows, out_w, ((1,), (1,))).astype(jnp.bfloat16)
    wide = kept * dim
    attended, dquery, dkey, dvalue = (
        v.reshape(total, wide)
        for v in attention(
            qkv[:, :wide].reshape(shape4),
            qkv[:, wide : 2 * wide].reshape(shape4),
            qkv[:, 2 * wide :].reshape(shape4),
            dattn.reshape(shape4),
            scale,
        )
    )
    dqkv = jnp.concatenate([dquery, dkey, dvalue], axis=1)
    grad_out = matmul(attended, full_drows, ((0,), (0,))).astype(jnp.bfloat16)
    grad_in = matmul(full_rows, dqkv, ((0,), (0,))).astype(jnp.bfloat16)
    partial_x = matmul(dqkv, full_w, ((1,), (1,))).astype(jnp.bfloat16)

    blocks = grad_in.reshape(lines, width // lines, 3 * wide)
    summed = pick(blocks, a).astype(jnp.float32)
    for s in range(1, lines):
        summed = summed + grid.shift(pick(blocks, (a + s) % lines), s).astype(jnp.float32)
    summed = summed.astype(jnp.bfloat16).reshape(2, 2, shard, 3 * wide)
    parts = {}
    for db in range(2):
        for dy in range(2):
            for dc in range(2):
                block = pick(pick(summed, b ^ db), c ^ dc)
                parts[db, dy, dc] = block if db + dy + dc == 0 else grid.flip(block, db, dc, dy)
    square = jnp.stack([parts[db, dy, dc] for db in range(2) for dy in range(2) for dc in range(2)])
    own = 4 * b + 2 * y + c
    square = jnp.stack([pick(square, own ^ at) for at in range(8)])
    square = square.reshape(2, 2, 2, shard, 3, kept, dim).transpose(3, 4, 2, 5, 0, 1, 6)
    grads_in = square.reshape(shard, 3 * width).astype(jnp.float32)

    if one_head:
        blocks = grad_out.reshape(kept, dim, width)

        def head_for(line):
            return pick(blocks, jnp.clip(line - span * c, 0, kept - 1))

        summed = head_for(a).astype(jnp.float32)
        for s in range(1, lines):
            summed = summed + grid.send(
                head_for((a + s) % lines),
                lambda a, b, c, g, y: (
                    ((a + s) % lines, b, c, g, y) if ((a + s) % lines) // span == c else None
                ),
            ).astype(jnp.float32)
        summed = summed.astype(jnp.bfloat16)
        grads_out = grid.send(
            summed, lambda a, b, c, g, y: (a, b, y, g, y) if a // span == c else None
        ) + grid.send(summed, lambda a, b, c, g, y: (a, b, y, g, y ^ 1) if a // span == c else None)
        grads_out = grads_out.astype(jnp.float32)
    else:
        whole = jnp.zeros((2, kept, 2, 2, dim, width), jnp.float32)
        at = (c, 0, b, y, 0, 0)
        whole = lax.dynamic_update_slice(
            whole, grad_out.astype(jnp.float32).reshape(1, kept, 1, 1, dim, width), at
        ).reshape(width, width)
        pairs = [[2 * g, 2 * g + 1] for g in range(grid.groups)]
        whole = lax.psum(whole, "rep", axis_index_groups=pairs)
        grads_out = lax.psum_scatter(whole, "pix", scatter_dimension=0, tiled=True)
    grads = jnp.concatenate([grads_in, grads_out], axis=1)
    if grid.groups > 1:
        same = [[2 * g + y for g in range(grid.groups)] for y in range(2)]
        grads = lax.psum(grads, "rep", axis_index_groups=same)

    chunks = partial_x.reshape(2, 4, count, width)
    pair = chunks[0].astype(jnp.float32) + grid.flip(chunks[1], 0, 1, 0).astype(jnp.float32)
    sent = pair.astype(jnp.bfloat16)
    dinput = pair[0]
    for at, (db, dy) in enumerate(((1, 0), (0, 1), (1, 1))):
        dinput = dinput + grid.flip(sent[at + 1], db, 0, dy).astype(jnp.float32)
    return dinput.astype(jnp.bfloat16).reshape(tokens.shape), grads


def solution(mesh):
    pix, rep = mesh.shape["pix"], mesh.shape["rep"]
    sites = P(BOTH, None, None)
    rows = P("pix", None)

    def step(*operands):
        return local(pix, rep, *operands)

    return jax.shard_map(
        step,
        mesh=mesh,
        in_specs=(sites, sites, rows, rows, rows, rows),
        out_specs=(sites, rows),
        check_vma=False,
    )
```

```python
import functools

import jax
import jax.numpy as jnp
from jax import lax
from jax.experimental import pallas as pl
from jax.experimental.pallas import tpu as pltpu
from jax.sharding import PartitionSpec as P

HEADS = 16
FRAMES = 16
KEPT = 2
BLOCK = 256
BOTH = ("pix", "rep")
VMEM = pl.BlockSpec(memory_space=pltpu.VMEM)
SMEM = pl.BlockSpec(memory_space=pltpu.SMEM)


def matmul(left, right, dims):
    return lax.dot_general(left, right, (dims, ((), ())), preferred_element_type=jnp.float32)


def shape_of(*dims, dtype=jnp.bfloat16):
    return jax.ShapeDtypeStruct(dims, dtype)


class Grid:
    def __init__(self, pix, rep):
        self.lines, self.groups, self.rep = pix // 4, rep // 2, rep

    def all(self):
        for a in range(self.lines):
            for b in range(2):
                for c in range(2):
                    for g in range(self.groups):
                        for y in range(2):
                            yield a, b, c, g, y

    def flat(self, a, b, c, g, y):
        return (4 * a + 2 * b + c) * self.rep + 2 * g + y

    def send(self, value, target):
        pairs = []
        for source in self.all():
            to = target(*source)
            if to is not None:
                pairs.append((self.flat(*source), self.flat(*to)))
        return lax.ppermute(value, BOTH, pairs)

    def flip(self, value, db, dc, dy):
        return self.send(value, lambda a, b, c, g, y: (a, b ^ db, c ^ dc, g, y ^ dy))


def pack_kernel(dim, at_ref, *refs):
    *weights, out_ref = refs
    even = at_ref[3] == 0
    values = [ref[...] for ref in weights]
    for b in range(2):
        for c in range(2):
            pieces = []
            for value in values:
                for k in range(KEPT):
                    low = (8 * c + 4 * k + 2 * b) * dim
                    first, second = value[:, low : low + dim], value[:, low + dim : low + 2 * dim]
                    pieces.append(jnp.where(even, first, second))
            block = jnp.concatenate(pieces, axis=1)
            for a in range(out_ref.shape[0] // 4):
                out_ref[4 * a + 2 * b + c] = block


def attend(query, keyed, valued, dattn, scale):
    rows = query.shape[0]
    site = lambda axis: lax.broadcasted_iota(jnp.int32, (rows, rows), axis) // FRAMES
    scores = matmul(query, keyed, ((1,), (1,))) * scale
    scores = jnp.where(site(0) == site(1), scores, -1e30)
    expo = jnp.exp(scores - jnp.max(scores, axis=1, keepdims=True))
    probs = expo / jnp.sum(expo, axis=1, keepdims=True)
    probs_b = probs.astype(jnp.bfloat16)
    attended = matmul(probs_b, valued, ((1,), (0,)))
    dvalue = matmul(probs_b, dattn, ((0,), (0,)))
    dprobs = matmul(dattn, valued, ((1,), (1,)))
    inner = jnp.sum(dprobs * probs, axis=1, keepdims=True)
    dscore = (probs * (dprobs - inner) * scale).astype(jnp.bfloat16)
    dquery = matmul(dscore, keyed, ((1,), (0,)))
    dkey = matmul(dscore, query, ((0,), (0,)))
    return [v.astype(jnp.bfloat16) for v in (attended, dquery, dkey, dvalue)]


def attention_kernel(scale, sub, at_ref, *refs):
    xs, xc, ds, dc, w_ref, out_w = refs[:6]
    grad_in, grad_out, dqkv_ref = refs[6:9]
    full, att, grads = refs[9:]
    shard, wide = w_ref.shape[1:]
    dim = wide // (3 * KEPT)
    width = xs.shape[-1]
    for p in range(w_ref.shape[0]):
        full[p * shard : (p + 1) * shard, :] = w_ref[p]
    half = xs.shape[0] * xs.shape[1]
    each = BLOCK // xs.shape[1]
    for part, (x_ref, d_ref) in enumerate(((xs, ds), (xc, dc))):

        def block(j, _, part=part, x_ref=x_ref, d_ref=d_ref):
            x = x_ref[pl.ds(each * j, each)].reshape(BLOCK, width)
            d = d_ref[pl.ds(each * j, each)].reshape(BLOCK, width)
            qkv = matmul(x, full[...], ((1,), (0,))).astype(jnp.bfloat16)
            da = matmul(d, out_w[...], ((1,), (1,))).astype(jnp.bfloat16)
            row = pl.multiple_of(part * half + j * BLOCK, BLOCK)
            for low in range(0, BLOCK, sub):
                outs = []
                for k in range(KEPT):
                    cut = lambda v, n: v[low : low + sub, n * dim : (n + 1) * dim]
                    outs.append(
                        attend(
                            cut(qkv, k), cut(qkv, KEPT + k), cut(qkv, 2 * KEPT + k), cut(da, k), scale
                        )
                    )
                att[pl.ds(row + low, sub), :] = jnp.concatenate([o[0] for o in outs], axis=1)
                dqkv_ref[pl.ds(row + low, sub), :] = jnp.concatenate(
                    [outs[k][n] for n in (1, 2, 3) for k in range(KEPT)], axis=1
                )
            return 0

        lax.fori_loop(0, half // BLOCK, block, 0)

    def columns(m, _):
        at = pl.multiple_of(m * 128, 128)
        first = matmul(att[:half, :], ds[:, :, pl.ds(at, 128)].reshape(half, 128), ((0,), (0,)))
        second = matmul(att[half:, :], dc[:, :, pl.ds(at, 128)].reshape(half, 128), ((0,), (0,)))
        grad_out[:, pl.ds(at, 128)] = (first + second).astype(jnp.bfloat16)
        first = matmul(xs[:, :, pl.ds(at, 128)].reshape(half, 128), dqkv_ref[:half, :], ((0,), (0,)))
        second = matmul(xc[:, :, pl.ds(at, 128)].reshape(half, 128), dqkv_ref[half:, :], ((0,), (0,)))
        grads[pl.ds(at, 128), :] = first + second
        return 0

    lax.fori_loop(0, width // 128, columns, 0)
    for p in range(w_ref.shape[0]):
        grad_in[p] = grads[p * shard : (p + 1) * shard, :].astype(jnp.bfloat16)


def input_kernel(dqkv_ref, w_ref, own_ref, other_ref, full):
    shard = w_ref.shape[1]
    for p in range(w_ref.shape[0]):
        full[p * shard : (p + 1) * shard, :] = w_ref[p]
    chunks, count, width = own_ref.shape
    each = BLOCK // count
    for part, out in enumerate((own_ref, other_ref)):

        def block(j, _, part=part, out=out):
            row = pl.multiple_of((part * chunks + each * j) * count, BLOCK)
            value = matmul(dqkv_ref[pl.ds(row, BLOCK), :], full[...], ((1,), (1,)))
            out[pl.ds(each * j, each)] = value.astype(jnp.bfloat16).reshape(each, count, width)
            return 0

        lax.fori_loop(0, chunks // each, block, 0)


def spread_kernel(dim, at_ref, own_ref, other_ref, kept_ref, moved_ref, out_ref):
    even = at_ref[3] == 0
    width = HEADS * dim
    for b in range(2):
        for c in range(2):
            own, other = own_ref[2 * b + c], other_ref[2 * b + c]
            first = jnp.where(even, own, other).astype(jnp.float32)
            second = jnp.where(even, other, own).astype(jnp.float32)
            for w in range(3):
                for k in range(KEPT):
                    piece = slice((w * KEPT + k) * dim, (w * KEPT + k + 1) * dim)
                    low = w * width + (8 * c + 4 * k + 2 * b) * dim
                    both = jnp.concatenate([first[:, piece], second[:, piece]], axis=1)
                    out_ref[:, low : low + 2 * dim] = both
    out_ref[:, 3 * width :] = kept_ref[...].astype(jnp.float32) + moved_ref[...].astype(jnp.float32)


def local(pix, rep, tokens, out_grad, query_weight, key_weight, value_weight, output_weight):
    grid = Grid(pix, rep)
    lines = grid.lines
    width = tokens.shape[-1]
    dim = width // HEADS
    wide = KEPT * dim
    shard = query_weight.shape[0]
    scale = 1.0 / dim**0.5
    place, rank = lax.axis_index("pix"), lax.axis_index("rep")
    a, b, c, y = place // 4, (place // 2) % 2, place % 2, rank % 2
    at = jnp.stack([a, b, c, y]).astype(jnp.int32)
    rows = tokens.reshape(-1, width)
    drows = out_grad.reshape(-1, width)
    count = rows.shape[0]
    total = 8 * count

    def gather_rows(own):
        chips = jnp.stack([own] + [grid.flip(own, db, 0, dy) for db, dy in ((1, 0), (0, 1), (1, 1))])
        return chips, grid.flip(chips, 0, 1, 0)

    packed = pl.pallas_call(
        functools.partial(pack_kernel, dim),
        out_shape=shape_of(pix, shard, 3 * wide),
        in_specs=[SMEM, VMEM, VMEM, VMEM],
        out_specs=VMEM,
    )(at, query_weight, key_weight, value_weight)
    xs, xc = gather_rows(rows)
    weights = lax.all_to_all(packed, "pix", 0, 0, tiled=True)

    one_head = shard == dim
    span = lines // 2
    if one_head:
        heads = jnp.stack(
            [
                grid.send(
                    output_weight,
                    lambda a, b, c, g, y: (
                        ((a + s) % lines, b, a // span, g, y) if c == y else None
                    ),
                )
                for s in range(lines)
            ]
        )
        out_w = jnp.concatenate(
            [
                lax.dynamic_index_in_dim(heads, (a - span * c - k) % lines, 0, keepdims=False)
                for k in range(KEPT)
            ],
            axis=0,
        )
    else:
        everything = lax.all_gather(output_weight, "pix", axis=0, tiled=True)
        everything = everything.reshape(2, KEPT, 2, 2, dim, width)
        out_w = lax.dynamic_index_in_dim(everything, c, 0, keepdims=False)
        out_w = lax.dynamic_index_in_dim(
            out_w.reshape(KEPT, 4, dim, width), 2 * b + y, 1, keepdims=False
        ).reshape(wide, width)
    ds, dc = gather_rows(drows)

    grad_in, grad_out, dqkv = pl.pallas_call(
        functools.partial(attention_kernel, scale, 128),
        out_shape=(shape_of(pix, shard, 3 * wide), shape_of(wide, width), shape_of(total, 3 * wide)),
        in_specs=[SMEM] + [VMEM] * 6,
        out_specs=(VMEM,) * 3,
        scratch_shapes=[
            pltpu.VMEM((width, 3 * wide), jnp.bfloat16),
            pltpu.VMEM((total, wide), jnp.bfloat16),
            pltpu.VMEM((width, 3 * wide), jnp.float32),
        ],
        cost_estimate=pl.CostEstimate(
            flops=8 * total * width * wide * 2, bytes_accessed=10 << 20, transcendentals=total * 32
        ),
    )(at, xs, xc, ds, dc, weights, out_w)

    received = lax.all_to_all(grad_in, "pix", 0, 0, tiled=True)
    summed = received.reshape(lines, 4, shard, 3 * wide).astype(jnp.float32).sum(0).astype(jnp.bfloat16)
    swapped = grid.flip(summed, 0, 0, 1)

    if one_head:
        blocks = grad_out.reshape(KEPT, dim, width)
        partial = [
            grid.send(
                lax.dynamic_index_in_dim(
                    blocks, jnp.clip((a + s) % lines - span * c, 0, KEPT - 1), 0, keepdims=False
                ),
                lambda a, b, c, g, y: (
                    ((a + s) % lines, b, y, g, y) if ((a + s) % lines) // span == c else None
                ),
            )
            for s in range(lines)
        ]
        kept = sum(p.astype(jnp.float32) for p in partial).astype(jnp.bfloat16)
        moved = grid.send(kept, lambda a, b, c, g, y: (a, b, c, g, y ^ 1) if c == y else None)
    else:
        whole = jnp.zeros((2, KEPT, 2, 2, dim, width), jnp.float32)
        whole = lax.dynamic_update_slice(
            whole,
            grad_out.astype(jnp.float32).reshape(1, KEPT, 1, 1, dim, width),
            (c, 0, b, y, 0, 0),
        ).reshape(width, width)
        pairs = [[2 * g, 2 * g + 1] for g in range(grid.groups)]
        whole = lax.psum(whole, "rep", axis_index_groups=pairs)
        kept = lax.psum_scatter(whole, "pix", scatter_dimension=0, tiled=True)
        moved = jnp.zeros_like(kept)

    own_part, other_part = pl.pallas_call(
        input_kernel,
        out_shape=(shape_of(4, count, width),) * 2,
        in_specs=[VMEM] * 2,
        out_specs=(VMEM,) * 2,
        scratch_shapes=[pltpu.VMEM((width, 3 * wide), jnp.bfloat16)],
        cost_estimate=pl.CostEstimate(
            flops=6 * total * width * wide, bytes_accessed=8 << 20, transcendentals=0
        ),
    )(dqkv, weights)
    pair = own_part.astype(jnp.float32) + grid.flip(other_part, 0, 1, 0).astype(jnp.float32)
    sent = pair.astype(jnp.bfloat16)
    dinput = pair[0]
    for i, (db, dy) in enumerate(((1, 0), (0, 1), (1, 1))):
        dinput = dinput + grid.flip(sent[i + 1], db, 0, dy).astype(jnp.float32)

    grads = pl.pallas_call(
        functools.partial(spread_kernel, dim),
        out_shape=shape_of(shard, 4 * width, dtype=jnp.float32),
        in_specs=[SMEM] + [VMEM] * 4,
        out_specs=VMEM,
    )(at, summed, swapped, kept, moved)
    if grid.groups > 1:
        same = [[2 * g + y for g in range(grid.groups)] for y in range(2)]
        grads = lax.psum(grads, "rep", axis_index_groups=same)
    return dinput.astype(jnp.bfloat16).reshape(tokens.shape), grads


def solution(mesh):
    pix, rep = mesh.shape["pix"], mesh.shape["rep"]
    sites = P(BOTH, None, None)
    rows = P("pix", None)

    def step(*operands):
        return local(pix, rep, *operands)

    return jax.shard_map(
        step,
        mesh=mesh,
        in_specs=(sites, sites, rows, rows, rows, rows),
        out_specs=(sites, rows),
        check_vma=False,
    )
```

```python
import functools

import jax
import jax.numpy as jnp
from jax import lax
from jax.experimental import pallas as pl
from jax.experimental.pallas import tpu as pltpu
from jax.sharding import PartitionSpec as P


HEADS = 16
FRAMES = 16
KEPT = 2
BLOCK = 256
BOTH = ("pix", "rep")
VMEM = pl.BlockSpec(memory_space=pltpu.VMEM)
SMEM = pl.BlockSpec(memory_space=pltpu.SMEM)


def matmul(left, right, dims):
    return lax.dot_general(left, right, (dims, ((), ())), preferred_element_type=jnp.float32)


def shape_of(*dims, dtype=jnp.bfloat16):
    return jax.ShapeDtypeStruct(dims, dtype)


class Grid:
    def __init__(self, pix, rep):
        self.lines, self.groups, self.rep = pix // 4, rep // 2, rep

    def all(self):
        for a in range(self.lines):
            for b in range(2):
                for c in range(2):
                    for g in range(self.groups):
                        for y in range(2):
                            yield a, b, c, g, y

    def flat(self, a, b, c, g, y):
        return (4 * a + 2 * b + c) * self.rep + 2 * g + y

    def send(self, value, target):
        pairs = []
        for source in self.all():
            to = target(*source)
            if to is not None:
                pairs.append((self.flat(*source), self.flat(*to)))
        return lax.ppermute(value, BOTH, pairs)

    def flip(self, value, db, dc, dy):
        return self.send(value, lambda a, b, c, g, y: (a, b ^ db, c ^ dc, g, y ^ dy))

    def shift(self, value, step):
        return self.send(value, lambda a, b, c, g, y: ((a + step) % self.lines, b, c, g, y))

    def gather_lines(self, value):
        lines = self.lines
        found = {0: value}
        for s in range(1, lines):
            if lines == 2 or 1 < s < lines - 1:
                found[s] = self.shift(value, s)
        if lines > 2:
            last = lines - 1
            step = lambda by: (
                lambda a, b, c, g, y: (a + by, b, c, g, y) if 0 <= a + by < lines else None
            )
            up = self.send(value, step(1))
            down = self.send(value, step(-1))
            if lines == 4:
                ends = self.send(
                    found[2],
                    lambda a, b, c, g, y: (
                        (3, b, c, g, y) if a == 2 else (0, b, c, g, y) if a == 1 else None
                    ),
                )
            else:
                ends = self.send(
                    value, lambda a, b, c, g, y: (last - a, b, c, g, y) if a in (0, last) else None
                )
            found[1], found[last], found[lines] = up, down, ends
        return [found[s] for s in range(len(found))]


def pack_kernel(dim, at_ref, *refs):
    weights, outs = refs[:3], refs[3:]
    even, b_here, c_here = at_ref[3] == 0, at_ref[1], at_ref[2]
    values = [ref[...] for ref in weights]
    for b in range(2):
        for c in range(2):
            pieces = []
            for value in values:
                for k in range(KEPT):
                    low = (8 * c + 4 * k + 2 * b) * dim
                    first, second = value[:, low : low + dim], value[:, low + dim : low + 2 * dim]
                    pieces.append(jnp.where(even, first, second))
            block = jnp.concatenate(pieces, axis=1)
            for db in range(2):
                for dc in range(2):

                    @pl.when((b_here == b ^ db) & (c_here == c ^ dc))
                    def _(db=db, dc=dc):
                        outs[2 * db + dc][...] = block


def plane_kernel(at_ref, *refs):
    *pieces, out_ref = refs
    here = 2 * at_ref[1] + at_ref[2]
    for n, piece in enumerate(pieces):
        out_ref[here ^ n] = piece[...]


def sum_kernel(at_ref, *refs):
    parts, outs = refs[: len(refs) - 4], refs[len(refs) - 4 :]
    here = 2 * at_ref[1] + at_ref[2]
    for n, out in enumerate(outs):
        out[...] = sum(p[here ^ n].astype(jnp.float32) for p in parts).astype(jnp.bfloat16)


def attend(query, keyed, valued, dattn, scale):
    rows = query.shape[0]
    site = lambda axis: lax.broadcasted_iota(jnp.int32, (rows, rows), axis) // FRAMES
    scores = matmul(query, keyed, ((1,), (1,))) * scale
    scores = jnp.where(site(0) == site(1), scores, -1e30)
    expo = jnp.exp(scores - jnp.max(scores, axis=1, keepdims=True))
    probs = expo / jnp.sum(expo, axis=1, keepdims=True)
    probs_b = probs.astype(jnp.bfloat16)
    attended = matmul(probs_b, valued, ((1,), (0,)))
    dvalue = matmul(probs_b, dattn, ((0,), (0,)))
    dprobs = matmul(dattn, valued, ((1,), (1,)))
    inner = jnp.sum(dprobs * probs, axis=1, keepdims=True)
    dscore = (probs * (dprobs - inner) * scale).astype(jnp.bfloat16)
    dquery = matmul(dscore, keyed, ((1,), (0,)))
    dkey = matmul(dscore, query, ((0,), (0,)))
    return [v.astype(jnp.bfloat16) for v in (attended, dquery, dkey, dvalue)]


def full_weights(lines, at_ref, planes, loose, full):
    def store(plane, line):
        for n in range(4):
            loose[4 * line + n] = plane[n]

    last = lines - 1
    for s in range(lines):
        line = lax.rem(at_ref[0] + lines - s, lines)
        if lines > 2 and s in (1, last):
            edge = at_ref[0] == (0 if s == 1 else last)
            pl.when(edge)(functools.partial(store, planes[lines], line))
            pl.when(jnp.logical_not(edge))(functools.partial(store, planes[s], line))
        else:
            store(planes[s], line)
    shard = loose.shape[1]
    for p in range(4 * lines):
        full[p * shard : (p + 1) * shard, :] = loose[p]


def attention_kernel(scale, sub, lines, at_ref, *refs):
    xs, xc, ds, dc = refs[:4]
    moved = 4 + lines + (lines > 2)
    planes, out_ws = refs[4:moved], refs[moved : len(refs) - lines - 7]
    grads_in = refs[len(refs) - lines - 7 : len(refs) - 7]
    grad_out, dqkv_ref, full, loose, out_w, att, grads = refs[len(refs) - 7 :]
    shard, wide = loose.shape[1:]
    dim = wide // (3 * KEPT)
    width = xs.shape[-1]
    full_weights(lines, at_ref, planes, loose, full)
    if len(out_ws) == 1:
        out_w[...] = out_ws[0][...]
    else:
        for s, held in enumerate(out_ws):
            line = lax.rem(at_ref[0] + lines - s, lines)
            for k in range(KEPT):

                @pl.when(line == KEPT * at_ref[2] + k)
                def _(k=k, held=held):
                    out_w[k * dim : (k + 1) * dim, :] = held[...]

    half = xs.shape[0] * xs.shape[1]
    each = BLOCK // xs.shape[1]
    for part, (x_ref, d_ref) in enumerate(((xs, ds), (xc, dc))):

        def block(j, _, part=part, x_ref=x_ref, d_ref=d_ref):
            x = x_ref[pl.ds(each * j, each)].reshape(BLOCK, width)
            d = d_ref[pl.ds(each * j, each)].reshape(BLOCK, width)
            qkv = matmul(x, full[...], ((1,), (0,))).astype(jnp.bfloat16)
            da = matmul(d, out_w[...], ((1,), (1,))).astype(jnp.bfloat16)
            row = pl.multiple_of(part * half + j * BLOCK, BLOCK)
            for low in range(0, BLOCK, sub):
                outs = []
                for k in range(KEPT):
                    cut = lambda v, n: v[low : low + sub, n * dim : (n + 1) * dim]
                    outs.append(
                        attend(
                            cut(qkv, k), cut(qkv, KEPT + k), cut(qkv, 2 * KEPT + k), cut(da, k), scale
                        )
                    )
                att[pl.ds(row + low, sub), :] = jnp.concatenate([o[0] for o in outs], axis=1)
                dqkv_ref[pl.ds(row + low, sub), :] = jnp.concatenate(
                    [outs[k][n] for n in (1, 2, 3) for k in range(KEPT)], axis=1
                )
            return 0

        lax.fori_loop(0, half // BLOCK, block, 0)

    def columns(m, _):
        at = pl.multiple_of(m * 128, 128)
        first = matmul(att[:half, :], ds[:, :, pl.ds(at, 128)].reshape(half, 128), ((0,), (0,)))
        second = matmul(att[half:, :], dc[:, :, pl.ds(at, 128)].reshape(half, 128), ((0,), (0,)))
        grad_out[:, pl.ds(at, 128)] = (first + second).astype(jnp.bfloat16)
        first = matmul(xs[:, :, pl.ds(at, 128)].reshape(half, 128), dqkv_ref[:half, :], ((0,), (0,)))
        second = matmul(xc[:, :, pl.ds(at, 128)].reshape(half, 128), dqkv_ref[half:, :], ((0,), (0,)))
        grads[pl.ds(at, 128), :] = first + second
        return 0

    lax.fori_loop(0, width // 128, columns, 0)
    for p in range(4 * lines):
        loose[p] = grads[p * shard : (p + 1) * shard, :].astype(jnp.bfloat16)
    for s, out in enumerate(grads_in):
        line = lax.rem(at_ref[0] + s, lines)
        for n in range(4):
            out[n] = loose[4 * line + n]


def input_kernel(lines, at_ref, dqkv_ref, *refs):
    *planes, own_ref, other_ref, full, loose = refs
    full_weights(lines, at_ref, planes, loose, full)
    chunks, count, width = own_ref.shape
    each = BLOCK // count
    for part, out in enumerate((own_ref, other_ref)):

        def block(j, _, part=part, out=out):
            row = pl.multiple_of((part * chunks + each * j) * count, BLOCK)
            value = matmul(dqkv_ref[pl.ds(row, BLOCK), :], full[...], ((1,), (1,)))
            out[pl.ds(each * j, each)] = value.astype(jnp.bfloat16).reshape(each, count, width)
            return 0

        lax.fori_loop(0, chunks // each, block, 0)


def spread_kernel(dim, at_ref, *refs):
    *pieces, kept_ref, moved_ref, out_ref, table = refs
    width = HEADS * dim
    for n, piece in enumerate(pieces):
        db, dc, dy = n // 4, (n // 2) % 2, n % 2
        b = lax.rem(at_ref[1] + db, 2)
        c = lax.rem(at_ref[2] + dc, 2)
        y = lax.rem(at_ref[3] + dy, 2)
        table[4 * b + 2 * c + y] = piece[...].astype(jnp.float32)
    for b in range(2):
        for c in range(2):
            first, second = table[4 * b + 2 * c], table[4 * b + 2 * c + 1]
            for w in range(3):
                for k in range(KEPT):
                    piece = slice((w * KEPT + k) * dim, (w * KEPT + k + 1) * dim)
                    low = w * width + (8 * c + 4 * k + 2 * b) * dim
                    both = jnp.concatenate([first[:, piece], second[:, piece]], axis=1)
                    out_ref[:, low : low + 2 * dim] = both
    out_ref[:, 3 * width :] = kept_ref[...].astype(jnp.float32) + moved_ref[...].astype(jnp.float32)


def local(pix, rep, tokens, out_grad, query_weight, key_weight, value_weight, output_weight):
    grid = Grid(pix, rep)
    lines = grid.lines
    width = tokens.shape[-1]
    dim = width // HEADS
    wide = KEPT * dim
    shard = query_weight.shape[0]
    scale = 1.0 / dim**0.5
    place, rank = lax.axis_index("pix"), lax.axis_index("rep")
    a, b, c, y = place // 4, (place // 2) % 2, place % 2, rank % 2
    at = jnp.stack([a, b, c, y]).astype(jnp.int32)
    rows = tokens.reshape(-1, width)
    drows = out_grad.reshape(-1, width)
    count = rows.shape[0]
    total = 8 * count

    def gather_rows(own):
        ways = ((1, 0), (0, 1), (1, 1))
        chips = jnp.stack([own] + [grid.flip(own, db, 0, dy) for db, dy in ways])
        return chips, grid.flip(chips, 0, 1, 0)

    pieces = pl.pallas_call(
        functools.partial(pack_kernel, dim),
        out_shape=(shape_of(shard, 3 * wide),) * 4,
        in_specs=[SMEM, VMEM, VMEM, VMEM],
        out_specs=(VMEM,) * 4,
    )(at, query_weight, key_weight, value_weight)
    pieces = [pieces[0]] + [grid.flip(pieces[n], n // 2, n % 2, 0) for n in range(1, 4)]
    plane = pl.pallas_call(
        plane_kernel,
        out_shape=shape_of(4, shard, 3 * wide),
        in_specs=[SMEM] + [VMEM] * 4,
        out_specs=VMEM,
    )(at, *pieces)
    xs, xc = gather_rows(rows)
    planes = grid.gather_lines(plane)

    one_head = shard == dim
    span = lines // 2
    if one_head:
        out_ws = [
            grid.send(
                output_weight,
                lambda a, b, c, g, y: (((a + s) % lines, b, a // span, g, y) if c == y else None),
            )
            for s in range(lines)
        ]
    else:
        everything = lax.all_gather(output_weight, "pix", axis=0, tiled=True)
        everything = everything.reshape(2, KEPT, 2, 2, dim, width)
        out_w = lax.dynamic_index_in_dim(everything, c, 0, keepdims=False)
        out_w = lax.dynamic_index_in_dim(
            out_w.reshape(KEPT, 4, dim, width), 2 * b + y, 1, keepdims=False
        ).reshape(wide, width)
        out_ws = [out_w]
    ds, dc = gather_rows(drows)

    *grads_in, grad_out, dqkv = pl.pallas_call(
        functools.partial(attention_kernel, scale, 128, lines),
        out_shape=(shape_of(4, shard, 3 * wide),) * lines
        + (shape_of(wide, width), shape_of(total, 3 * wide)),
        in_specs=[SMEM] + [VMEM] * (4 + len(planes) + len(out_ws)),
        out_specs=(VMEM,) * (lines + 2),
        scratch_shapes=[
            pltpu.VMEM((width, 3 * wide), jnp.bfloat16),
            pltpu.VMEM((pix, shard, 3 * wide), jnp.bfloat16),
            pltpu.VMEM((wide, width), jnp.bfloat16),
            pltpu.VMEM((total, wide), jnp.bfloat16),
            pltpu.VMEM((width, 3 * wide), jnp.float32),
        ],
        cost_estimate=pl.CostEstimate(
            flops=8 * total * width * wide * 2, bytes_accessed=10 << 20, transcendentals=total * 32
        ),
    )(at, xs, xc, ds, dc, *planes, *out_ws)

    summed = pl.pallas_call(
        sum_kernel,
        out_shape=(shape_of(shard, 3 * wide),) * 4,
        in_specs=[SMEM] + [VMEM] * lines,
        out_specs=(VMEM,) * 4,
    )(at, grads_in[0], *[grid.shift(grads_in[s], s) for s in range(1, lines)])
    square = []
    for n in range(8):
        block = summed[n // 2]
        square.append(grid.flip(block, n // 4, (n // 2) % 2, n % 2) if n else block)

    if one_head:
        blocks = grad_out.reshape(KEPT, dim, width)
        partial = [
            grid.send(
                lax.dynamic_index_in_dim(
                    blocks, jnp.clip((a + s) % lines - span * c, 0, KEPT - 1), 0, keepdims=False
                ),
                lambda a, b, c, g, y: (
                    ((a + s) % lines, b, y, g, y) if ((a + s) % lines) // span == c else None
                ),
            )
            for s in range(lines)
        ]
        kept = sum(p.astype(jnp.float32) for p in partial).astype(jnp.bfloat16)
        moved = grid.send(kept, lambda a, b, c, g, y: (a, b, c, g, y ^ 1) if c == y else None)
    else:
        whole = jnp.zeros((2, KEPT, 2, 2, dim, width), jnp.float32)
        whole = lax.dynamic_update_slice(
            whole,
            grad_out.astype(jnp.float32).reshape(1, KEPT, 1, 1, dim, width),
            (c, 0, b, y, 0, 0),
        ).reshape(width, width)
        pairs = [[2 * g, 2 * g + 1] for g in range(grid.groups)]
        whole = lax.psum(whole, "rep", axis_index_groups=pairs)
        kept = lax.psum_scatter(whole, "pix", scatter_dimension=0, tiled=True)
        moved = jnp.zeros_like(kept)

    input_call = pl.pallas_call(
        functools.partial(input_kernel, lines),
        out_shape=(shape_of(4, count, width),) * 2,
        in_specs=[SMEM] + [VMEM] * (1 + len(planes)),
        out_specs=(VMEM,) * 2,
        scratch_shapes=[
            pltpu.VMEM((width, 3 * wide), jnp.bfloat16),
            pltpu.VMEM((pix, shard, 3 * wide), jnp.bfloat16),
        ],
        cost_estimate=pl.CostEstimate(
            flops=6 * total * width * wide, bytes_accessed=8 << 20, transcendentals=0
        ),
    )
    own_part, other_part = input_call(at, dqkv, *planes)
    pair = own_part.astype(jnp.float32) + grid.flip(other_part, 0, 1, 0).astype(jnp.float32)
    sent = pair.astype(jnp.bfloat16)
    dinput = pair[0]
    for i, (db, dy) in enumerate(((1, 0), (0, 1), (1, 1))):
        dinput = dinput + grid.flip(sent[i + 1], db, 0, dy).astype(jnp.float32)

    grads = pl.pallas_call(
        functools.partial(spread_kernel, dim),
        out_shape=shape_of(shard, 4 * width, dtype=jnp.float32),
        in_specs=[SMEM] + [VMEM] * 10,
        out_specs=VMEM,
        scratch_shapes=[pltpu.VMEM((8, shard, 3 * wide), jnp.float32)],
    )(at, *square, kept, moved)
    if grid.groups > 1:
        same = [[2 * g + y for g in range(grid.groups)] for y in range(2)]
        grads = lax.psum(grads, "rep", axis_index_groups=same)
    return dinput.astype(jnp.bfloat16).reshape(tokens.shape), grads


def solution(mesh):
    pix, rep = mesh.shape["pix"], mesh.shape["rep"]
    sites = P(BOTH, None, None)
    rows = P("pix", None)

    def step(*operands):
        return local(pix, rep, *operands)

    return jax.shard_map(
        step,
        mesh=mesh,
        in_specs=(sites, sites, rows, rows, rows, rows),
        out_specs=(sites, rows),
        check_vma=False,
    )
```

```python
import functools

import jax
import jax.numpy as jnp
from jax import lax
from jax.experimental import pallas as pl
from jax.experimental.pallas import tpu as pltpu
from jax.sharding import PartitionSpec as P


HEADS = 16
FRAMES = 16
KEPT = 2
BLOCK = 256
BOTH = ("pix", "rep")
VMEM = pl.BlockSpec(memory_space=pltpu.VMEM)
SMEM = pl.BlockSpec(memory_space=pltpu.SMEM)


def room(mib):
    return pltpu.CompilerParams(vmem_limit_bytes=mib << 20)


def matmul(left, right, dims):
    return lax.dot_general(left, right, (dims, ((), ())), preferred_element_type=jnp.float32)


def shape_of(*dims, dtype=jnp.bfloat16):
    return jax.ShapeDtypeStruct(dims, dtype)


class Grid:
    def __init__(self, pix, rep):
        self.lines, self.groups, self.rep = pix // 4, rep // 2, rep

    def all(self):
        for a in range(self.lines):
            for b in range(2):
                for c in range(2):
                    for g in range(self.groups):
                        for y in range(2):
                            yield a, b, c, g, y

    def flat(self, a, b, c, g, y):
        return (4 * a + 2 * b + c) * self.rep + 2 * g + y

    def send(self, value, target):
        pairs = []
        for source in self.all():
            to = target(*source)
            if to is not None:
                pairs.append((self.flat(*source), self.flat(*to)))
        return lax.ppermute(value, BOTH, pairs)

    def flip(self, value, db, dc, dy):
        return self.send(value, lambda a, b, c, g, y: (a, b ^ db, c ^ dc, g, y ^ dy))

    def shift(self, value, step):
        return self.send(value, lambda a, b, c, g, y: ((a + step) % self.lines, b, c, g, y))

    def gather_lines(self, value):
        lines = self.lines
        found = {0: value}
        for s in range(1, lines):
            if lines == 2 or 1 < s < lines - 1:
                found[s] = self.shift(value, s)
        if lines > 2:
            last = lines - 1
            step = lambda by: (
                lambda a, b, c, g, y: (a + by, b, c, g, y) if 0 <= a + by < lines else None
            )
            up = self.send(value, step(1))
            down = self.send(value, step(-1))
            if lines == 4:
                ends = self.send(
                    found[2],
                    lambda a, b, c, g, y: (
                        (3, b, c, g, y) if a == 2 else (0, b, c, g, y) if a == 1 else None
                    ),
                )
            else:
                ends = self.send(
                    value, lambda a, b, c, g, y: (last - a, b, c, g, y) if a in (0, last) else None
                )
            found[1], found[last], found[lines] = up, down, ends
        return [found[s] for s in range(len(found))]


def pack_kernel(dim, at_ref, *refs):
    weights, outs = refs[:3], refs[3:]
    even, b_here, c_here = at_ref[3] == 0, at_ref[1], at_ref[2]
    values = [ref[...] for ref in weights]
    for b in range(2):
        for c in range(2):
            pieces = []
            for value in values:
                for k in range(KEPT):
                    low = (8 * c + 4 * k + 2 * b) * dim
                    first, second = value[:, low : low + dim], value[:, low + dim : low + 2 * dim]
                    pieces.append(jnp.where(even, first, second))
            block = jnp.concatenate(pieces, axis=1)
            for db in range(2):
                for dc in range(2):

                    @pl.when((b_here == b ^ db) & (c_here == c ^ dc))
                    def _(db=db, dc=dc):
                        outs[2 * db + dc][...] = block


def plane_kernel(at_ref, *refs):
    *pieces, out_ref = refs
    here = 2 * at_ref[1] + at_ref[2]
    for n, piece in enumerate(pieces):
        out_ref[here ^ n] = piece[...]


def sum_kernel(at_ref, *refs):
    parts, outs = refs[: len(refs) - 4], refs[len(refs) - 4 :]
    here = 2 * at_ref[1] + at_ref[2]
    for n, out in enumerate(outs):
        out[...] = sum(p[here ^ n].astype(jnp.float32) for p in parts).astype(jnp.bfloat16)


def attend(query, keyed, valued, dattn, scale):
    rows = query.shape[0]
    site = lambda axis: lax.broadcasted_iota(jnp.int32, (rows, rows), axis) // FRAMES
    scores = matmul(query, keyed, ((1,), (1,))) * scale
    scores = jnp.where(site(0) == site(1), scores, -1e30)
    expo = jnp.exp(scores - jnp.max(scores, axis=1, keepdims=True))
    probs = expo / jnp.sum(expo, axis=1, keepdims=True)
    probs_b = probs.astype(jnp.bfloat16)
    attended = matmul(probs_b, valued, ((1,), (0,)))
    dvalue = matmul(probs_b, dattn, ((0,), (0,)))
    dprobs = matmul(dattn, valued, ((1,), (1,)))
    inner = jnp.sum(dprobs * probs, axis=1, keepdims=True)
    dscore = (probs * (dprobs - inner) * scale).astype(jnp.bfloat16)
    dquery = matmul(dscore, keyed, ((1,), (0,)))
    dkey = matmul(dscore, query, ((0,), (0,)))
    return [v.astype(jnp.bfloat16) for v in (attended, dquery, dkey, dvalue)]


def full_weights(lines, at_ref, planes, loose, full):
    def store(plane, line):
        for n in range(4):
            loose[4 * line + n] = plane[n]

    last = lines - 1
    for s in range(lines):
        line = lax.rem(at_ref[0] + lines - s, lines)
        if lines > 2 and s in (1, last):
            edge = at_ref[0] == (0 if s == 1 else last)
            pl.when(edge)(functools.partial(store, planes[lines], line))
            pl.when(jnp.logical_not(edge))(functools.partial(store, planes[s], line))
        else:
            store(planes[s], line)
    shard = loose.shape[1]
    for p in range(4 * lines):
        full[p * shard : (p + 1) * shard, :] = loose[p]


def attention_kernel(scale, sub, lines, at_ref, *refs):
    xs, xc, ds, dc = refs[:4]
    moved = 4 + lines + (lines > 2)
    planes, out_ws = refs[4:moved], refs[moved : len(refs) - lines - 7]
    grads_in = refs[len(refs) - lines - 7 : len(refs) - 7]
    grad_out, dqkv_ref, full, loose, out_w, att, grads = refs[len(refs) - 7 :]
    shard, wide = loose.shape[1:]
    dim = wide // (3 * KEPT)
    width = xs.shape[-1]
    full_weights(lines, at_ref, planes, loose, full)
    if len(out_ws) == 1:
        out_w[...] = out_ws[0][...]
    else:
        for s, held in enumerate(out_ws):
            line = lax.rem(at_ref[0] + lines - s, lines)
            for k in range(KEPT):

                @pl.when(line == KEPT * at_ref[2] + k)
                def _(k=k, held=held):
                    out_w[k * dim : (k + 1) * dim, :] = held[...]

    half = xs.shape[0] * xs.shape[1]
    each = BLOCK // xs.shape[1]
    for part, (x_ref, d_ref) in enumerate(((xs, ds), (xc, dc))):

        def block(j, _, part=part, x_ref=x_ref, d_ref=d_ref):
            x = x_ref[pl.ds(each * j, each)].reshape(BLOCK, width)
            d = d_ref[pl.ds(each * j, each)].reshape(BLOCK, width)
            qkv = matmul(x, full[...], ((1,), (0,))).astype(jnp.bfloat16)
            da = matmul(d, out_w[...], ((1,), (1,))).astype(jnp.bfloat16)
            row = pl.multiple_of(part * half + j * BLOCK, BLOCK)
            for low in range(0, BLOCK, sub):
                outs = []
                for k in range(KEPT):
                    cut = lambda v, n: v[low : low + sub, n * dim : (n + 1) * dim]
                    outs.append(
                        attend(
                            cut(qkv, k), cut(qkv, KEPT + k), cut(qkv, 2 * KEPT + k), cut(da, k), scale
                        )
                    )
                att[pl.ds(row + low, sub), :] = jnp.concatenate([o[0] for o in outs], axis=1)
                dqkv_ref[pl.ds(row + low, sub), :] = jnp.concatenate(
                    [outs[k][n] for n in (1, 2, 3) for k in range(KEPT)], axis=1
                )
            return 0

        lax.fori_loop(0, half // BLOCK, block, 0)

    def columns(m, _):
        at = pl.multiple_of(m * 128, 128)
        first = matmul(att[:half, :], ds[:, :, pl.ds(at, 128)].reshape(half, 128), ((0,), (0,)))
        second = matmul(att[half:, :], dc[:, :, pl.ds(at, 128)].reshape(half, 128), ((0,), (0,)))
        grad_out[:, pl.ds(at, 128)] = (first + second).astype(jnp.bfloat16)
        first = matmul(xs[:, :, pl.ds(at, 128)].reshape(half, 128), dqkv_ref[:half, :], ((0,), (0,)))
        second = matmul(xc[:, :, pl.ds(at, 128)].reshape(half, 128), dqkv_ref[half:, :], ((0,), (0,)))
        grads[pl.ds(at, 128), :] = first + second
        return 0

    lax.fori_loop(0, width // 128, columns, 0)
    for p in range(4 * lines):
        loose[p] = grads[p * shard : (p + 1) * shard, :].astype(jnp.bfloat16)
    for s, out in enumerate(grads_in):
        line = lax.rem(at_ref[0] + s, lines)
        for n in range(4):
            out[n] = loose[4 * line + n]


def input_kernel(lines, at_ref, dqkv_ref, *refs):
    *planes, own_ref, other_ref, full, loose = refs
    full_weights(lines, at_ref, planes, loose, full)
    chunks, count, width = own_ref.shape
    each = BLOCK // count
    for part, out in enumerate((own_ref, other_ref)):

        def block(j, _, part=part, out=out):
            row = pl.multiple_of((part * chunks + each * j) * count, BLOCK)
            value = matmul(dqkv_ref[pl.ds(row, BLOCK), :], full[...], ((1,), (1,)))
            out[pl.ds(each * j, each)] = value.astype(jnp.bfloat16).reshape(each, count, width)
            return 0

        lax.fori_loop(0, chunks // each, block, 0)


def spread_kernel(dim, at_ref, *refs):
    *pieces, kept_ref, moved_ref, out_ref, table = refs
    width = HEADS * dim
    for n, piece in enumerate(pieces):
        db, dc, dy = n // 4, (n // 2) % 2, n % 2
        b = lax.rem(at_ref[1] + db, 2)
        c = lax.rem(at_ref[2] + dc, 2)
        y = lax.rem(at_ref[3] + dy, 2)
        table[4 * b + 2 * c + y] = piece[...].astype(jnp.float32)
    for b in range(2):
        for c in range(2):
            first, second = table[4 * b + 2 * c], table[4 * b + 2 * c + 1]
            for w in range(3):
                for k in range(KEPT):
                    piece = slice((w * KEPT + k) * dim, (w * KEPT + k + 1) * dim)
                    low = w * width + (8 * c + 4 * k + 2 * b) * dim
                    both = jnp.concatenate([first[:, piece], second[:, piece]], axis=1)
                    out_ref[:, low : low + 2 * dim] = both
    out_ref[:, 3 * width :] = kept_ref[...].astype(jnp.float32) + moved_ref[...].astype(jnp.float32)


def local(pix, rep, tokens, out_grad, query_weight, key_weight, value_weight, output_weight):
    grid = Grid(pix, rep)
    lines = grid.lines
    width = tokens.shape[-1]
    dim = width // HEADS
    wide = KEPT * dim
    shard = query_weight.shape[0]
    scale = 1.0 / dim**0.5
    place, rank = lax.axis_index("pix"), lax.axis_index("rep")
    a, b, c, y = place // 4, (place // 2) % 2, place % 2, rank % 2
    at = jnp.stack([a, b, c, y]).astype(jnp.int32)
    rows = tokens.reshape(-1, width)
    drows = out_grad.reshape(-1, width)
    count = rows.shape[0]
    total = 8 * count

    def gather_rows(own):
        ways = ((1, 0), (0, 1), (1, 1))
        chips = jnp.stack([own] + [grid.flip(own, db, 0, dy) for db, dy in ways])
        return chips, grid.flip(chips, 0, 1, 0)

    pieces = pl.pallas_call(
        functools.partial(pack_kernel, dim),
        compiler_params=room(8),
        out_shape=(shape_of(shard, 3 * wide),) * 4,
        in_specs=[SMEM, VMEM, VMEM, VMEM],
        out_specs=(VMEM,) * 4,
    )(at, query_weight, key_weight, value_weight)
    pieces = [pieces[0]] + [grid.flip(pieces[n], n // 2, n % 2, 0) for n in range(1, 4)]
    plane = pl.pallas_call(
        plane_kernel,
        compiler_params=room(8),
        out_shape=shape_of(4, shard, 3 * wide),
        in_specs=[SMEM] + [VMEM] * 4,
        out_specs=VMEM,
    )(at, *pieces)
    xs, xc = gather_rows(rows)
    planes = grid.gather_lines(plane)

    one_head = shard == dim
    span = lines // 2
    if one_head:
        out_ws = [
            grid.send(
                output_weight,
                lambda a, b, c, g, y: (((a + s) % lines, b, a // span, g, y) if c == y else None),
            )
            for s in range(lines)
        ]
    else:
        everything = lax.all_gather(output_weight, "pix", axis=0, tiled=True)
        everything = everything.reshape(2, KEPT, 2, 2, dim, width)
        out_w = lax.dynamic_index_in_dim(everything, c, 0, keepdims=False)
        out_w = lax.dynamic_index_in_dim(
            out_w.reshape(KEPT, 4, dim, width), 2 * b + y, 1, keepdims=False
        ).reshape(wide, width)
        out_ws = [out_w]
    ds, dc = gather_rows(drows)

    *grads_in, grad_out, dqkv = pl.pallas_call(
        functools.partial(attention_kernel, scale, BLOCK, lines),
        compiler_params=room(28),
        out_shape=(shape_of(4, shard, 3 * wide),) * lines
        + (shape_of(wide, width), shape_of(total, 3 * wide)),
        in_specs=[SMEM] + [VMEM] * (4 + len(planes) + len(out_ws)),
        out_specs=(VMEM,) * (lines + 2),
        scratch_shapes=[
            pltpu.VMEM((width, 3 * wide), jnp.bfloat16),
            pltpu.VMEM((pix, shard, 3 * wide), jnp.bfloat16),
            pltpu.VMEM((wide, width), jnp.bfloat16),
            pltpu.VMEM((total, wide), jnp.bfloat16),
            pltpu.VMEM((width, 3 * wide), jnp.float32),
        ],
        cost_estimate=pl.CostEstimate(
            flops=8 * total * width * wide * 2, bytes_accessed=10 << 20, transcendentals=total * 32
        ),
    )(at, xs, xc, ds, dc, *planes, *out_ws)

    summed = pl.pallas_call(
        sum_kernel,
        compiler_params=room(8),
        out_shape=(shape_of(shard, 3 * wide),) * 4,
        in_specs=[SMEM] + [VMEM] * lines,
        out_specs=(VMEM,) * 4,
    )(at, grads_in[0], *[grid.shift(grads_in[s], s) for s in range(1, lines)])
    square = []
    for n in range(8):
        block = summed[n // 2]
        square.append(grid.flip(block, n // 4, (n // 2) % 2, n % 2) if n else block)

    if one_head:
        blocks = grad_out.reshape(KEPT, dim, width)
        partial = [
            grid.send(
                lax.dynamic_index_in_dim(
                    blocks, jnp.clip((a + s) % lines - span * c, 0, KEPT - 1), 0, keepdims=False
                ),
                lambda a, b, c, g, y: (
                    ((a + s) % lines, b, y, g, y) if ((a + s) % lines) // span == c else None
                ),
            )
            for s in range(lines)
        ]
        kept = sum(p.astype(jnp.float32) for p in partial).astype(jnp.bfloat16)
        moved = grid.send(kept, lambda a, b, c, g, y: (a, b, c, g, y ^ 1) if c == y else None)
    else:
        whole = jnp.zeros((2, KEPT, 2, 2, dim, width), jnp.float32)
        whole = lax.dynamic_update_slice(
            whole,
            grad_out.astype(jnp.float32).reshape(1, KEPT, 1, 1, dim, width),
            (c, 0, b, y, 0, 0),
        ).reshape(width, width)
        pairs = [[2 * g, 2 * g + 1] for g in range(grid.groups)]
        whole = lax.psum(whole, "rep", axis_index_groups=pairs)
        kept = lax.psum_scatter(whole, "pix", scatter_dimension=0, tiled=True)
        moved = jnp.zeros_like(kept)

    input_call = pl.pallas_call(
        functools.partial(input_kernel, lines),
        compiler_params=room(20),
        out_shape=(shape_of(4, count, width),) * 2,
        in_specs=[SMEM] + [VMEM] * (1 + len(planes)),
        out_specs=(VMEM,) * 2,
        scratch_shapes=[
            pltpu.VMEM((width, 3 * wide), jnp.bfloat16),
            pltpu.VMEM((pix, shard, 3 * wide), jnp.bfloat16),
        ],
        cost_estimate=pl.CostEstimate(
            flops=6 * total * width * wide, bytes_accessed=8 << 20, transcendentals=0
        ),
    )
    own_part, other_part = input_call(at, dqkv, *planes)
    pair = own_part.astype(jnp.float32) + grid.flip(other_part, 0, 1, 0).astype(jnp.float32)
    sent = pair.astype(jnp.bfloat16)
    moves = [
        grid.flip(sent[i + 1], db, 0, dy)
        for i, (db, dy) in enumerate(((1, 0), (0, 1), (1, 1)))
    ]
    dinput = pair[0] + sum(move.astype(jnp.float32) for move in moves)
    dinput = dinput.astype(jnp.bfloat16)

    grads = pl.pallas_call(
        functools.partial(spread_kernel, dim),
        compiler_params=room(12),
        out_shape=shape_of(shard, 4 * width, dtype=jnp.float32),
        in_specs=[SMEM] + [VMEM] * 10,
        out_specs=VMEM,
        scratch_shapes=[pltpu.VMEM((8, shard, 3 * wide), jnp.float32)],
    )(at, *square, kept, moved)
    if grid.groups > 1:
        same = [[2 * g + y for g in range(grid.groups)] for y in range(2)]
        grads = lax.psum(grads, "rep", axis_index_groups=same)
    return dinput.reshape(tokens.shape), grads


def solution(mesh):
    pix, rep = mesh.shape["pix"], mesh.shape["rep"]
    sites = P(BOTH, None, None)
    rows = P("pix", None)

    def step(*operands):
        return local(pix, rep, *operands)

    return jax.shard_map(
        step,
        mesh=mesh,
        in_specs=(sites, sites, rows, rows, rows, rows),
        out_specs=(sites, rows),
        check_vma=False,
    )
```

```python
import functools

import jax
import jax.numpy as jnp
from jax import lax
from jax.experimental import pallas as pl
from jax.experimental.pallas import tpu as pltpu
from jax.sharding import PartitionSpec as P


HEADS = 16
FRAMES = 16
KEPT = 2
BLOCK = 256
BOTH = ("pix", "rep")
VMEM = pl.BlockSpec(memory_space=pltpu.VMEM)
SMEM = pl.BlockSpec(memory_space=pltpu.SMEM)


def room(mib):
    return pltpu.CompilerParams(vmem_limit_bytes=mib << 20)


def matmul(left, right, dims):
    return lax.dot_general(left, right, (dims, ((), ())), preferred_element_type=jnp.float32)


def shape_of(*dims, dtype=jnp.bfloat16):
    return jax.ShapeDtypeStruct(dims, dtype)


class Grid:
    def __init__(self, pix, rep):
        self.lines, self.groups, self.rep = pix // 4, rep // 2, rep

    def all(self):
        for a in range(self.lines):
            for b in range(2):
                for c in range(2):
                    for g in range(self.groups):
                        for y in range(2):
                            yield a, b, c, g, y

    def flat(self, a, b, c, g, y):
        return (4 * a + 2 * b + c) * self.rep + 2 * g + y

    def send(self, value, target):
        pairs = []
        for source in self.all():
            to = target(*source)
            if to is not None:
                pairs.append((self.flat(*source), self.flat(*to)))
        return lax.ppermute(value, BOTH, pairs)

    def flip(self, value, db, dc, dy):
        return self.send(value, lambda a, b, c, g, y: (a, b ^ db, c ^ dc, g, y ^ dy))

    def shift(self, value, step):
        return self.send(value, lambda a, b, c, g, y: ((a + step) % self.lines, b, c, g, y))

    def gather_lines(self, value):
        lines = self.lines
        found = {0: value}
        for s in range(1, lines):
            if lines == 2 or 1 < s < lines - 1:
                found[s] = self.shift(value, s)
        if lines > 2:
            last = lines - 1
            step = lambda by: (
                lambda a, b, c, g, y: (a + by, b, c, g, y) if 0 <= a + by < lines else None
            )
            up = self.send(value, step(1))
            down = self.send(value, step(-1))
            if lines == 4:
                ends = self.send(
                    found[2],
                    lambda a, b, c, g, y: (
                        (3, b, c, g, y) if a == 2 else (0, b, c, g, y) if a == 1 else None
                    ),
                )
            else:
                ends = self.send(
                    value, lambda a, b, c, g, y: (last - a, b, c, g, y) if a in (0, last) else None
                )
            found[1], found[last], found[lines] = up, down, ends
        return [found[s] for s in range(len(found))]

    def scatter_lines(self, values):
        lines = self.lines
        if lines != 4:
            return [values[0]] + [self.shift(values[s], s) for s in range(1, lines)]

        def way(hops):
            return lambda a, b, c, g, y: (hops[a], b, c, g, y) if a in hops else None

        relay = self.send(values[4], way({0: 1, 3: 2}))
        terms = [
            values[0],
            self.send(values[2], way({0: 2, 3: 1})),
            self.send(values[1], way({0: 1, 1: 2, 2: 3})),
            self.send(values[3], way({1: 0, 2: 1, 3: 2})),
        ]
        both = values[2].astype(jnp.float32) + relay.astype(jnp.float32)
        return terms + [self.send(both.astype(jnp.bfloat16), way({1: 3, 2: 0}))]


def pack_kernel(dim, at_ref, *refs):
    sources, outs, weights, sems = refs[:3], refs[3:7], refs[7:10], refs[10]
    copies = [pltpu.make_async_copy(sources[w], weights[w], sems.at[w]) for w in range(3)]
    for copy in copies:
        copy.start()
    for copy in copies:
        copy.wait()
    even, b_here, c_here = at_ref[3] == 0, at_ref[1], at_ref[2]
    values = [ref[...] for ref in weights]
    for b in range(2):
        for c in range(2):
            pieces = []
            for value in values:
                for k in range(KEPT):
                    low = (8 * c + 4 * k + 2 * b) * dim
                    first, second = value[:, low : low + dim], value[:, low + dim : low + 2 * dim]
                    pieces.append(jnp.where(even, first, second))
            block = jnp.concatenate(pieces, axis=1)
            for db in range(2):
                for dc in range(2):

                    @pl.when((b_here == b ^ db) & (c_here == c ^ dc))
                    def _(db=db, dc=dc):
                        outs[2 * db + dc][...] = block


def plane_kernel(at_ref, *refs):
    *pieces, out_ref = refs
    here = 2 * at_ref[1] + at_ref[2]
    wide = pieces[0].shape[1]
    for n, piece in enumerate(pieces):
        index = here ^ n
        for side in range(2):

            @pl.when(index % 2 == side)
            def _(side=side, piece=piece, index=index):
                out_ref[index // 2, :, side * wide : (side + 1) * wide] = piece[...]


def sum_kernel(at_ref, *refs):
    parts, outs = refs[: len(refs) - 4], refs[len(refs) - 4 :]
    here = 2 * at_ref[1] + at_ref[2]
    wide = outs[0].shape[1]
    for n, out in enumerate(outs):
        index = here ^ n
        for side in range(2):

            @pl.when(index % 2 == side)
            def _(side=side, out=out, index=index):
                cut = slice(side * wide, (side + 1) * wide)
                total = sum(p[index // 2, :, cut].astype(jnp.float32) for p in parts)
                out[...] = total.astype(jnp.bfloat16)


def attend(query, keyed, valued, dattn, scale, bias):
    scores = matmul(query, keyed, ((1,), (1,))) * scale + bias
    expo = jnp.exp(scores - jnp.max(scores, axis=1, keepdims=True))
    probs = expo * (1.0 / jnp.sum(expo, axis=1, keepdims=True))
    probs_b = probs.astype(jnp.bfloat16)
    attended = matmul(probs_b, valued, ((1,), (0,)))
    dvalue = matmul(probs_b, dattn, ((0,), (0,)))
    dprobs = matmul(dattn, valued, ((1,), (1,)))
    inner = jnp.sum(dprobs * probs, axis=1, keepdims=True)
    dscore = (probs * (dprobs - inner) * scale).astype(jnp.bfloat16)
    dquery = matmul(dscore, keyed, ((1,), (0,)))
    dkey = matmul(dscore, query, ((0,), (0,)))
    return [v.astype(jnp.bfloat16) for v in (attended, dquery, dkey, dvalue)]


def full_weights(lines, at_ref, planes, loose, full):
    def store(plane, line):
        for n in range(4):
            side = (n % 2) * loose.shape[2]
            loose[4 * line + n] = plane[n // 2, :, side : side + loose.shape[2]]

    last = lines - 1
    for s in range(lines):
        line = lax.rem(at_ref[0] + lines - s, lines)
        if lines > 2 and s in (1, last):
            edge = at_ref[0] == (0 if s == 1 else last)
            pl.when(edge)(functools.partial(store, planes[lines], line))
            pl.when(jnp.logical_not(edge))(functools.partial(store, planes[s], line))
        else:
            store(planes[s], line)
    shard = loose.shape[1]
    for p in range(4 * lines):
        full[p * shard : (p + 1) * shard, :] = loose[p]


def attention_kernel(scale, lines, at_ref, *refs):
    xs, xc, ds, dc = refs[:4]
    moved = 4 + lines + (lines > 2)
    sent = lines + (lines == 4)
    planes, out_ws = refs[4:moved], refs[moved : len(refs) - sent - 8]
    grads_in = refs[len(refs) - sent - 8 : len(refs) - 8]
    grad_out, dqkv_ref, full, loose, out_w, att, grads, bias = refs[len(refs) - 8 :]
    shard, wide = loose.shape[1:]
    dim = wide // (3 * KEPT)
    width = xs.shape[-1]
    full_weights(lines, at_ref, planes, loose, full)
    if len(out_ws) == 1:
        out_w[...] = out_ws[0][...]
    else:
        for s, held in enumerate(out_ws):
            line = lax.rem(at_ref[0] + lines - s, lines)
            for k in range(KEPT):

                @pl.when(line == KEPT * at_ref[2] + k)
                def _(k=k, held=held):
                    out_w[k * dim : (k + 1) * dim, :] = held[...]

    site = lambda axis: lax.broadcasted_iota(jnp.int32, (BLOCK, BLOCK), axis) // FRAMES
    bias[...] = jnp.where(site(0) == site(1), 0.0, -1e30)
    half = xs.shape[0] * xs.shape[1]
    each = BLOCK // xs.shape[1]
    for part, (x_ref, d_ref) in enumerate(((xs, ds), (xc, dc))):

        def block(j, _, part=part, x_ref=x_ref, d_ref=d_ref):
            x = x_ref[pl.ds(each * j, each)].reshape(BLOCK, width)
            d = d_ref[pl.ds(each * j, each)].reshape(BLOCK, width)
            qkv = matmul(x, full[...], ((1,), (0,))).astype(jnp.bfloat16)
            da = matmul(d, out_w[...], ((1,), (1,))).astype(jnp.bfloat16)
            row = pl.multiple_of(part * half + j * BLOCK, BLOCK)
            cut = lambda v, n: v[:, n * dim : (n + 1) * dim]
            outs = [
                attend(
                    cut(qkv, k),
                    cut(qkv, KEPT + k),
                    cut(qkv, 2 * KEPT + k),
                    cut(da, k),
                    scale,
                    bias[...],
                )
                for k in range(KEPT)
            ]
            att[pl.ds(row, BLOCK), :] = jnp.concatenate([o[0] for o in outs], axis=1)
            dqkv_ref[pl.ds(row, BLOCK), :] = jnp.concatenate(
                [outs[k][n] for n in (1, 2, 3) for k in range(KEPT)], axis=1
            )
            return 0

        lax.fori_loop(0, half // BLOCK, block, 0)

    def columns(m, _):
        at = pl.multiple_of(m * 128, 128)
        first = matmul(att[:half, :], ds[:, :, pl.ds(at, 128)].reshape(half, 128), ((0,), (0,)))
        second = matmul(att[half:, :], dc[:, :, pl.ds(at, 128)].reshape(half, 128), ((0,), (0,)))
        grad_out[:, pl.ds(at, 128)] = (first + second).astype(jnp.bfloat16)
        first = matmul(xs[:, :, pl.ds(at, 128)].reshape(half, 128), dqkv_ref[:half, :], ((0,), (0,)))
        second = matmul(xc[:, :, pl.ds(at, 128)].reshape(half, 128), dqkv_ref[half:, :], ((0,), (0,)))
        grads[pl.ds(at, 128), :] = first + second
        return 0

    lax.fori_loop(0, width // 128, columns, 0)
    for p in range(4 * lines):
        loose[p] = grads[p * shard : (p + 1) * shard, :].astype(jnp.bfloat16)
    for s, out in enumerate(grads_in):
        line = lax.rem(at_ref[0] + s, lines)
        if s == lines:
            line = jnp.where(at_ref[0] == 0, lines - 1, 0)
        for n in range(4):
            out[n // 2, :, (n % 2) * wide : (n % 2 + 1) * wide] = loose[4 * line + n]


def input_kernel(lines, at_ref, dqkv_ref, *refs):
    *planes, own_ref, other_ref, full, loose = refs
    full_weights(lines, at_ref, planes, loose, full)
    chunks, count, width = own_ref.shape
    each = BLOCK // count
    for part, out in enumerate((own_ref, other_ref)):

        def block(j, _, part=part, out=out):
            row = pl.multiple_of((part * chunks + each * j) * count, BLOCK)
            value = matmul(dqkv_ref[pl.ds(row, BLOCK), :], full[...], ((1,), (1,)))
            out[pl.ds(each * j, each)] = value.astype(jnp.bfloat16).reshape(each, count, width)
            return 0

        lax.fori_loop(0, chunks // each, block, 0)


def spread_kernel(dim, at_ref, *refs):
    *pieces, kept_ref, moved_ref, out_ref, table = refs
    step = pl.program_id(0)

    @pl.when(step == 0)
    def _():
        for n, piece in enumerate(pieces):
            db, dc, dy = n // 4, (n // 2) % 2, n % 2
            b = lax.rem(at_ref[1] + db, 2)
            c = lax.rem(at_ref[2] + dc, 2)
            y = lax.rem(at_ref[3] + dy, 2)
            table[4 * b + 2 * c + y] = piece[...]
        out_ref[...] = kept_ref[...].astype(jnp.float32) + moved_ref[...].astype(jnp.float32)

    for w in range(3):

        @pl.when(step == w + 1)
        def _(w=w):
            heads = []
            for h in range(HEADS):
                c, k, b, y = h // 8, (h // 4) % 2, (h // 2) % 2, h % 2
                low = (w * KEPT + k) * dim
                heads.append(table[4 * b + 2 * c + y, :, low : low + dim].astype(jnp.float32))
            out_ref[...] = jnp.concatenate(heads, axis=1)


def local(pix, rep, tokens, out_grad, query_weight, key_weight, value_weight, output_weight):
    grid = Grid(pix, rep)
    lines = grid.lines
    width = tokens.shape[-1]
    dim = width // HEADS
    wide = KEPT * dim
    shard = query_weight.shape[0]
    scale = 1.0 / dim**0.5
    place, rank = lax.axis_index("pix"), lax.axis_index("rep")
    a, b, c, y = place // 4, (place // 2) % 2, place % 2, rank % 2
    at = jnp.stack([a, b, c, y]).astype(jnp.int32)
    rows = tokens.reshape(-1, width)
    drows = out_grad.reshape(-1, width)
    count = rows.shape[0]
    total = 8 * count

    def gather_rows(own):
        ways = ((1, 0), (0, 1), (1, 1))
        chips = jnp.stack([own] + [grid.flip(own, db, 0, dy) for db, dy in ways])
        return chips, grid.flip(chips, 0, 1, 0)

    pieces = pl.pallas_call(
        functools.partial(pack_kernel, dim),
        compiler_params=room(8),
        out_shape=(shape_of(shard, 3 * wide),) * 4,
        in_specs=[SMEM] + [pl.BlockSpec(memory_space=pltpu.HBM)] * 3,
        out_specs=(VMEM,) * 4,
        scratch_shapes=[pltpu.VMEM((shard, width), jnp.bfloat16)] * 3
        + [pltpu.SemaphoreType.DMA((3,))],
    )(at, query_weight, key_weight, value_weight)
    pieces = [pieces[0]] + [grid.flip(pieces[n], n // 2, n % 2, 0) for n in range(1, 4)]
    plane = pl.pallas_call(
        plane_kernel,
        compiler_params=room(8),
        out_shape=shape_of(2, shard, 6 * wide),
        in_specs=[SMEM] + [VMEM] * 4,
        out_specs=VMEM,
    )(at, *pieces)
    xs, xc = gather_rows(rows)
    planes = grid.gather_lines(plane)

    one_head = shard == dim
    span = lines // 2
    if one_head:
        out_ws = [
            grid.send(
                output_weight,
                lambda a, b, c, g, y: (((a + s) % lines, b, a // span, g, y) if c == y else None),
            )
            for s in range(lines)
        ]
    else:
        everything = lax.all_gather(output_weight, "pix", axis=0, tiled=True)
        everything = everything.reshape(2, KEPT, 2, 2, dim, width)
        out_w = lax.dynamic_index_in_dim(everything, c, 0, keepdims=False)
        out_w = lax.dynamic_index_in_dim(
            out_w.reshape(KEPT, 4, dim, width), 2 * b + y, 1, keepdims=False
        ).reshape(wide, width)
        out_ws = [out_w]
    ds, dc = gather_rows(drows)

    sent = lines + (lines == 4)
    *grads_in, grad_out, dqkv = pl.pallas_call(
        functools.partial(attention_kernel, scale, lines),
        compiler_params=room(28),
        out_shape=(shape_of(2, shard, 6 * wide),) * sent
        + (shape_of(wide, width), shape_of(total, 3 * wide)),
        in_specs=[SMEM] + [VMEM] * (4 + len(planes) + len(out_ws)),
        out_specs=(VMEM,) * (sent + 2),
        scratch_shapes=[
            pltpu.VMEM((width, 3 * wide), jnp.bfloat16),
            pltpu.VMEM((pix, shard, 3 * wide), jnp.bfloat16),
            pltpu.VMEM((wide, width), jnp.bfloat16),
            pltpu.VMEM((total, wide), jnp.bfloat16),
            pltpu.VMEM((width, 3 * wide), jnp.float32),
            pltpu.VMEM((BLOCK, BLOCK), jnp.float32),
        ],
        cost_estimate=pl.CostEstimate(
            flops=8 * total * width * wide * 2, bytes_accessed=10 << 20, transcendentals=total * 32
        ),
    )(at, xs, xc, ds, dc, *planes, *out_ws)

    parts = grid.scatter_lines(grads_in)
    summed = pl.pallas_call(
        sum_kernel,
        compiler_params=room(8),
        out_shape=(shape_of(shard, 3 * wide),) * 4,
        in_specs=[SMEM] + [VMEM] * len(parts),
        out_specs=(VMEM,) * 4,
    )(at, *parts)
    square = []
    for n in range(8):
        block = summed[n // 2]
        square.append(grid.flip(block, n // 4, (n // 2) % 2, n % 2) if n else block)

    if one_head:
        blocks = grad_out.reshape(KEPT, dim, width)
        partial = [
            grid.send(
                lax.dynamic_index_in_dim(
                    blocks, jnp.clip((a + s) % lines - span * c, 0, KEPT - 1), 0, keepdims=False
                ),
                lambda a, b, c, g, y: (
                    ((a + s) % lines, b, y, g, y) if ((a + s) % lines) // span == c else None
                ),
            )
            for s in range(lines)
        ]
        kept = sum(p.astype(jnp.float32) for p in partial).astype(jnp.bfloat16)
        moved = grid.send(kept, lambda a, b, c, g, y: (a, b, c, g, y ^ 1) if c == y else None)
    else:
        whole = jnp.zeros((2, KEPT, 2, 2, dim, width), jnp.float32)
        whole = lax.dynamic_update_slice(
            whole,
            grad_out.astype(jnp.float32).reshape(1, KEPT, 1, 1, dim, width),
            (c, 0, b, y, 0, 0),
        ).reshape(width, width)
        pairs = [[2 * g, 2 * g + 1] for g in range(grid.groups)]
        whole = lax.psum(whole, "rep", axis_index_groups=pairs)
        kept = lax.psum_scatter(whole, "pix", scatter_dimension=0, tiled=True)
        moved = jnp.zeros_like(kept)

    input_call = pl.pallas_call(
        functools.partial(input_kernel, lines),
        compiler_params=room(20),
        out_shape=(shape_of(4, count, width),) * 2,
        in_specs=[SMEM] + [VMEM] * (1 + len(planes)),
        out_specs=(VMEM,) * 2,
        scratch_shapes=[
            pltpu.VMEM((width, 3 * wide), jnp.bfloat16),
            pltpu.VMEM((pix, shard, 3 * wide), jnp.bfloat16),
        ],
        cost_estimate=pl.CostEstimate(
            flops=6 * total * width * wide, bytes_accessed=8 << 20, transcendentals=0
        ),
    )
    own_part, other_part = input_call(at, dqkv, *planes)
    pair = own_part.astype(jnp.float32) + grid.flip(other_part, 0, 1, 0).astype(jnp.float32)
    sent = pair.astype(jnp.bfloat16)
    moves = [
        grid.flip(sent[i + 1], db, 0, dy)
        for i, (db, dy) in enumerate(((1, 0), (0, 1), (1, 1)))
    ]
    dinput = pair[0] + sum(move.astype(jnp.float32) for move in moves)
    dinput = dinput.astype(jnp.bfloat16)

    grads = pl.pallas_call(
        functools.partial(spread_kernel, dim),
        compiler_params=room(12),
        out_shape=shape_of(shard, 4 * width, dtype=jnp.float32),
        grid=(4,),
        in_specs=[SMEM] + [VMEM] * 10,
        out_specs=pl.BlockSpec((shard, width), lambda i: (0, (i + 3) % 4)),
        scratch_shapes=[pltpu.VMEM((8, shard, 3 * wide), jnp.bfloat16)],
    )(at, *square, kept, moved)
    if grid.groups > 1:
        same = [[2 * g + y for g in range(grid.groups)] for y in range(2)]
        grads = lax.psum(grads, "rep", axis_index_groups=same)
    return dinput.reshape(tokens.shape), grads


def solution(mesh):
    pix, rep = mesh.shape["pix"], mesh.shape["rep"]
    sites = P(BOTH, None, None)
    rows = P("pix", None)

    def step(*operands):
        return local(pix, rep, *operands)

    return jax.shard_map(
        step,
        mesh=mesh,
        in_specs=(sites, sites, rows, rows, rows, rows),
        out_specs=(sites, rows),
        check_vma=False,
    )
```

```python
import functools

import jax
import jax.numpy as jnp
from jax import lax
from jax.experimental import pallas as pl
from jax.experimental.pallas import tpu as pltpu
from jax.sharding import PartitionSpec as P


HEADS = 16
FRAMES = 16
KEPT = 2
BLOCK = 256
BOTH = ("pix", "rep")
VMEM = pl.BlockSpec(memory_space=pltpu.VMEM)
SMEM = pl.BlockSpec(memory_space=pltpu.SMEM)


def room(mib):
    return pltpu.CompilerParams(vmem_limit_bytes=mib << 20)


def matmul(left, right, dims):
    return lax.dot_general(left, right, (dims, ((), ())), preferred_element_type=jnp.float32)


def shape_of(*dims, dtype=jnp.bfloat16):
    return jax.ShapeDtypeStruct(dims, dtype)


class Grid:
    def __init__(self, pix, rep):
        self.lines, self.groups, self.rep = pix // 4, rep // 2, rep

    def all(self):
        for a in range(self.lines):
            for b in range(2):
                for c in range(2):
                    for g in range(self.groups):
                        for y in range(2):
                            yield a, b, c, g, y

    def flat(self, a, b, c, g, y):
        return (4 * a + 2 * b + c) * self.rep + 2 * g + y

    def send(self, value, target):
        pairs = []
        for source in self.all():
            to = target(*source)
            if to is not None:
                pairs.append((self.flat(*source), self.flat(*to)))
        return lax.ppermute(value, BOTH, pairs)

    def flip(self, value, db, dc, dy):
        return self.send(value, lambda a, b, c, g, y: (a, b ^ db, c ^ dc, g, y ^ dy))

    def shift(self, value, step):
        return self.send(value, lambda a, b, c, g, y: ((a + step) % self.lines, b, c, g, y))

    def gather_lines(self, value):
        lines = self.lines
        found = {0: value}
        for s in range(1, lines):
            if lines == 2 or 1 < s < lines - 1:
                found[s] = self.shift(value, s)
        if lines > 2:
            last = lines - 1
            step = lambda by: (
                lambda a, b, c, g, y: (a + by, b, c, g, y) if 0 <= a + by < lines else None
            )
            up = self.send(value, step(1))
            down = self.send(value, step(-1))
            if lines == 4:
                ends = self.send(
                    found[2],
                    lambda a, b, c, g, y: (
                        (3, b, c, g, y) if a == 2 else (0, b, c, g, y) if a == 1 else None
                    ),
                )
            else:
                ends = self.send(
                    value, lambda a, b, c, g, y: (last - a, b, c, g, y) if a in (0, last) else None
                )
            found[1], found[last], found[lines] = up, down, ends
        return [found[s] for s in range(len(found))]

    def scatter_lines(self, values):
        lines = self.lines
        if lines != 4:
            return [values[0]] + [self.shift(values[s], s) for s in range(1, lines)]

        def way(hops):
            return lambda a, b, c, g, y: (hops[a], b, c, g, y) if a in hops else None

        relay = self.send(values[4], way({0: 1, 3: 2}))
        terms = [
            values[0],
            self.send(values[2], way({0: 2, 3: 1})),
            self.send(values[1], way({0: 1, 1: 2, 2: 3})),
            self.send(values[3], way({1: 0, 2: 1, 3: 2})),
        ]
        both = values[2].astype(jnp.float32) + relay.astype(jnp.float32)
        return terms + [self.send(both.astype(jnp.bfloat16), way({1: 3, 2: 0}))]


def pack_kernel(dim, at_ref, *refs):
    sources, outs, weights, sems = refs[:3], refs[3:7], refs[7:10], refs[10]
    copies = [pltpu.make_async_copy(sources[w], weights[w], sems.at[w]) for w in range(3)]
    for copy in copies:
        copy.start()
    for copy in copies:
        copy.wait()
    even, b_here, c_here = at_ref[3] == 0, at_ref[1], at_ref[2]
    values = [ref[...] for ref in weights]
    for b in range(2):
        for c in range(2):
            pieces = []
            for value in values:
                for k in range(KEPT):
                    low = (8 * c + 4 * k + 2 * b) * dim
                    first, second = value[:, low : low + dim], value[:, low + dim : low + 2 * dim]
                    pieces.append(jnp.where(even, first, second))
            block = jnp.concatenate(pieces, axis=1)
            for db in range(2):
                for dc in range(2):

                    @pl.when((b_here == b ^ db) & (c_here == c ^ dc))
                    def _(db=db, dc=dc):
                        outs[2 * db + dc][...] = block


def plane_kernel(at_ref, *refs):
    *pieces, out_ref = refs
    here = 2 * at_ref[1] + at_ref[2]
    wide = pieces[0].shape[1]
    for n, piece in enumerate(pieces):
        index = here ^ n
        for side in range(2):

            @pl.when(index % 2 == side)
            def _(side=side, piece=piece, index=index):
                out_ref[index // 2, :, side * wide : (side + 1) * wide] = piece[...]


def sum_kernel(terms, at_ref, *refs):
    parts, heads, outs = refs[:terms], refs[terms : len(refs) - 6], refs[len(refs) - 6 :]
    here = 2 * at_ref[1] + at_ref[2]
    wide = outs[0].shape[1]
    for n, out in enumerate(outs[:4]):
        index = here ^ n
        for side in range(2):

            @pl.when(index % 2 == side)
            def _(side=side, out=out, index=index):
                cut = slice(side * wide, (side + 1) * wide)
                total = sum(p[index // 2, :, cut].astype(jnp.float32) for p in parts)
                out[...] = total.astype(jnp.bfloat16)

    kept, other = outs[4:]
    kept[...] = sum(h[...].astype(jnp.float32) for h in heads).astype(kept.dtype)
    width = kept.shape[1]
    other[:, :width] = kept[...]
    other[:, width:] = outs[0][...]


def attend(query, keyed, valued, dattn, scale, bias):
    scores = matmul(query, keyed, ((1,), (1,))) * scale + bias
    expo = jnp.exp(scores - jnp.max(scores, axis=1, keepdims=True))
    probs = expo * (1.0 / jnp.sum(expo, axis=1, keepdims=True))
    probs_b = probs.astype(jnp.bfloat16)
    attended = matmul(probs_b, valued, ((1,), (0,)))
    dvalue = matmul(probs_b, dattn, ((0,), (0,)))
    dprobs = matmul(dattn, valued, ((1,), (1,)))
    inner = jnp.sum(dprobs * probs, axis=1, keepdims=True)
    dscore = (probs * (dprobs - inner) * scale).astype(jnp.bfloat16)
    dquery = matmul(dscore, keyed, ((1,), (0,)))
    dkey = matmul(dscore, query, ((0,), (0,)))
    return [v.astype(jnp.bfloat16) for v in (attended, dquery, dkey, dvalue)]


def full_weights(lines, at_ref, planes, loose, full):
    def store(plane, line):
        for n in range(4):
            side = (n % 2) * loose.shape[2]
            loose[4 * line + n] = plane[n // 2, :, side : side + loose.shape[2]]

    last = lines - 1
    for s in range(lines):
        line = lax.rem(at_ref[0] + lines - s, lines)
        if lines > 2 and s in (1, last):
            edge = at_ref[0] == (0 if s == 1 else last)
            pl.when(edge)(functools.partial(store, planes[lines], line))
            pl.when(jnp.logical_not(edge))(functools.partial(store, planes[s], line))
        else:
            store(planes[s], line)
    shard = loose.shape[1]
    for p in range(4 * lines):
        full[p * shard : (p + 1) * shard, :] = loose[p]


def attention_kernel(scale, lines, at_ref, *refs):
    xs, xc, ds, dc = refs[:4]
    moved = 4 + lines + (lines > 2)
    sent = lines + (lines == 4)
    owed = lines if len(refs) > moved + 1 + sent + 9 else 1
    planes, out_ws = refs[4:moved], refs[moved : moved + owed]
    grads_in = refs[moved + owed : moved + owed + sent]
    grads_out = refs[moved + owed + sent : moved + 2 * owed + sent]
    dqkv_ref, full, loose, out_w, att, grads, bias = refs[moved + 2 * owed + sent :]
    shard, wide = loose.shape[1:]
    dim = wide // (3 * KEPT)
    width = xs.shape[-1]
    full_weights(lines, at_ref, planes, loose, full)
    if len(out_ws) == 1:
        out_w[...] = out_ws[0][...]
    else:
        for s, held in enumerate(out_ws):
            line = lax.rem(at_ref[0] + lines - s, lines)
            for k in range(KEPT):

                @pl.when(line == KEPT * at_ref[2] + k)
                def _(k=k, held=held):
                    out_w[k * dim : (k + 1) * dim, :] = held[...]

    site = lambda axis: lax.broadcasted_iota(jnp.int32, (BLOCK, BLOCK), axis) // FRAMES
    bias[...] = jnp.where(site(0) == site(1), 0.0, -1e30)
    half = xs.shape[0] * xs.shape[1]
    each = BLOCK // xs.shape[1]
    for part, (x_ref, d_ref) in enumerate(((xs, ds), (xc, dc))):

        def block(j, _, part=part, x_ref=x_ref, d_ref=d_ref):
            x = x_ref[pl.ds(each * j, each)].reshape(BLOCK, width)
            d = d_ref[pl.ds(each * j, each)].reshape(BLOCK, width)
            qkv = matmul(x, full[...], ((1,), (0,))).astype(jnp.bfloat16)
            da = matmul(d, out_w[...], ((1,), (1,))).astype(jnp.bfloat16)
            row = pl.multiple_of(part * half + j * BLOCK, BLOCK)
            cut = lambda v, n: v[:, n * dim : (n + 1) * dim]
            outs = [
                attend(
                    cut(qkv, k),
                    cut(qkv, KEPT + k),
                    cut(qkv, 2 * KEPT + k),
                    cut(da, k),
                    scale,
                    bias[...],
                )
                for k in range(KEPT)
            ]
            att[pl.ds(row, BLOCK), :] = jnp.concatenate([o[0] for o in outs], axis=1)
            dqkv_ref[pl.ds(row, BLOCK), :] = jnp.concatenate(
                [outs[k][n] for n in (1, 2, 3) for k in range(KEPT)], axis=1
            )
            return 0

        lax.fori_loop(0, half // BLOCK, block, 0, unroll=True)

    def columns(m, _):
        at = pl.multiple_of(m * 128, 128)
        first = matmul(att[:half, :], ds[:, :, pl.ds(at, 128)].reshape(half, 128), ((0,), (0,)))
        second = matmul(att[half:, :], dc[:, :, pl.ds(at, 128)].reshape(half, 128), ((0,), (0,)))
        term = (first + second).astype(jnp.bfloat16)
        if owed == 1:
            grads_out[0][:, pl.ds(at, 128)] = term
        for s in range(owed if owed > 1 else 0):
            upper = lax.rem(at_ref[0] + s, lines) != KEPT * at_ref[2]
            grads_out[s][:, pl.ds(at, 128)] = jnp.where(upper, term[dim:], term[:dim])
        first = matmul(xs[:, :, pl.ds(at, 128)].reshape(half, 128), dqkv_ref[:half, :], ((0,), (0,)))
        second = matmul(xc[:, :, pl.ds(at, 128)].reshape(half, 128), dqkv_ref[half:, :], ((0,), (0,)))
        grads[pl.ds(at, 128), :] = first + second
        return 0

    lax.fori_loop(0, width // 128, columns, 0, unroll=True)
    for p in range(4 * lines):
        loose[p] = grads[p * shard : (p + 1) * shard, :].astype(jnp.bfloat16)
    for s, out in enumerate(grads_in):
        line = lax.rem(at_ref[0] + s, lines)
        if s == lines:
            line = jnp.where(at_ref[0] == 0, lines - 1, 0)
        for n in range(4):
            out[n // 2, :, (n % 2) * wide : (n % 2 + 1) * wide] = loose[4 * line + n]


def input_kernel(dqkv_ref, full, own_ref, other_ref):
    chunks, count, width = own_ref.shape
    each = BLOCK // count
    for part, out in enumerate((own_ref, other_ref)):

        def block(j, _, part=part, out=out):
            row = pl.multiple_of((part * chunks + each * j) * count, BLOCK)
            value = matmul(dqkv_ref[pl.ds(row, BLOCK), :], full[...], ((1,), (1,)))
            out[pl.ds(each * j, each)] = value.astype(jnp.bfloat16).reshape(each, count, width)
            return 0

        lax.fori_loop(0, chunks // each, block, 0, unroll=True)


def spread_kernel(dim, at_ref, *refs):
    *pieces, kept_ref, out_ref, table = refs
    step = pl.program_id(0)

    @pl.when(step == 0)
    def _():
        for n, piece in enumerate(pieces):
            db, dc, dy = n // 4, (n // 2) % 2, n % 2
            b = lax.rem(at_ref[1] + db, 2)
            c = lax.rem(at_ref[2] + dc, 2)
            y = lax.rem(at_ref[3] + dy, 2)
            table[4 * b + 2 * c + y] = piece[:, piece.shape[1] - table.shape[2] :]
        moved = pieces[1][:, : out_ref.shape[1]].astype(jnp.float32)
        out_ref[...] = kept_ref[...].astype(jnp.float32) + moved

    for w in range(3):

        @pl.when(step == w + 1)
        def _(w=w):
            heads = []
            for h in range(HEADS):
                c, k, b, y = h // 8, (h // 4) % 2, (h // 2) % 2, h % 2
                low = (w * KEPT + k) * dim
                heads.append(table[4 * b + 2 * c + y, :, low : low + dim].astype(jnp.float32))
            out_ref[...] = jnp.concatenate(heads, axis=1)


def local(pix, rep, tokens, out_grad, query_weight, key_weight, value_weight, output_weight):
    grid = Grid(pix, rep)
    lines = grid.lines
    width = tokens.shape[-1]
    dim = width // HEADS
    wide = KEPT * dim
    shard = query_weight.shape[0]
    scale = 1.0 / dim**0.5
    place, rank = lax.axis_index("pix"), lax.axis_index("rep")
    a, b, c, y = place // 4, (place // 2) % 2, place % 2, rank % 2
    at = jnp.stack([a, b, c, y]).astype(jnp.int32)
    rows = tokens.reshape(-1, width)
    drows = out_grad.reshape(-1, width)
    count = rows.shape[0]
    total = 8 * count

    def gather_rows(own):
        ways = ((1, 0), (0, 1), (1, 1))
        chips = jnp.stack([own] + [grid.flip(own, db, 0, dy) for db, dy in ways])
        return chips, grid.flip(chips, 0, 1, 0)

    pieces = pl.pallas_call(
        functools.partial(pack_kernel, dim),
        compiler_params=room(8),
        out_shape=(shape_of(shard, 3 * wide),) * 4,
        in_specs=[SMEM] + [pl.BlockSpec(memory_space=pltpu.HBM)] * 3,
        out_specs=(VMEM,) * 4,
        scratch_shapes=[pltpu.VMEM((shard, width), jnp.bfloat16)] * 3
        + [pltpu.SemaphoreType.DMA((3,))],
    )(at, *[pltpu.with_memory_space_constraint(v, pltpu.HBM) for v in (query_weight, key_weight, value_weight)])
    pieces = [pieces[0]] + [grid.flip(pieces[n], n // 2, n % 2, 0) for n in range(1, 4)]
    plane = pl.pallas_call(
        plane_kernel,
        compiler_params=room(8),
        out_shape=shape_of(2, shard, 6 * wide),
        in_specs=[SMEM] + [VMEM] * 4,
        out_specs=VMEM,
    )(at, *pieces)
    xs, xc = gather_rows(rows)
    planes = grid.gather_lines(plane)

    one_head = shard == dim
    span = lines // 2
    if one_head:
        out_ws = [
            grid.send(
                output_weight,
                lambda a, b, c, g, y: (((a + s) % lines, b, a // span, g, y) if c == y else None),
            )
            for s in range(lines)
        ]
    else:
        everything = lax.all_gather(output_weight, "pix", axis=0, tiled=True)
        everything = everything.reshape(2, KEPT, 2, 2, dim, width)
        out_w = lax.dynamic_index_in_dim(everything, c, 0, keepdims=False)
        out_w = lax.dynamic_index_in_dim(
            out_w.reshape(KEPT, 4, dim, width), 2 * b + y, 1, keepdims=False
        ).reshape(wide, width)
        out_ws = [out_w]
    ds, dc = gather_rows(drows)

    sent = lines + (lines == 4)
    owed = len(out_ws)
    head_rows = dim if one_head else wide
    *results, dqkv, full = pl.pallas_call(
        functools.partial(attention_kernel, scale, lines),
        compiler_params=room(28),
        out_shape=(shape_of(2, shard, 6 * wide),) * sent
        + (shape_of(head_rows, width),) * owed
        + (shape_of(total, 3 * wide), shape_of(width, 3 * wide)),
        in_specs=[SMEM] + [VMEM] * (4 + len(planes) + len(out_ws)),
        out_specs=(VMEM,) * (sent + owed + 2),
        scratch_shapes=[
            pltpu.VMEM((pix, shard, 3 * wide), jnp.bfloat16),
            pltpu.VMEM((wide, width), jnp.bfloat16),
            pltpu.VMEM((total, wide), jnp.bfloat16),
            pltpu.VMEM((width, 3 * wide), jnp.float32),
            pltpu.VMEM((BLOCK, BLOCK), jnp.float32),
        ],
        cost_estimate=pl.CostEstimate(
            flops=8 * total * width * wide * 2, bytes_accessed=10 << 20, transcendentals=total * 32
        ),
    )(at, xs, xc, ds, dc, *planes, *out_ws)

    grads_in, grads_out = results[:sent], results[sent:]
    parts = grid.scatter_lines(grads_in)
    if one_head:
        heads = [
            grid.send(
                grads_out[s],
                lambda a, b, c, g, y: (
                    ((a + s) % lines, b, y, g, y) if ((a + s) % lines) // span == c else None
                ),
            )
            for s in range(lines)
        ]
    else:
        whole = jnp.zeros((2, KEPT, 2, 2, dim, width), jnp.float32)
        whole = lax.dynamic_update_slice(
            whole,
            grads_out[0].astype(jnp.float32).reshape(1, KEPT, 1, 1, dim, width),
            (c, 0, b, y, 0, 0),
        ).reshape(width, width)
        heads = [lax.psum_scatter(whole, "pix", scatter_dimension=0, tiled=True)]
    *summed, kept, other = pl.pallas_call(
        functools.partial(sum_kernel, len(parts)),
        compiler_params=room(10),
        out_shape=(shape_of(shard, 3 * wide),) * 4
        + (shape_of(shard, width), shape_of(shard, width + 3 * wide)),
        in_specs=[SMEM] + [VMEM] * (len(parts) + len(heads)),
        out_specs=(VMEM,) * 6,
    )(at, *parts, *heads)
    square = []
    for n in range(8):
        block = other if n == 1 else summed[n // 2]
        square.append(grid.flip(block, n // 4, (n // 2) % 2, n % 2) if n else block)

    input_call = pl.pallas_call(
        input_kernel,
        compiler_params=room(20),
        out_shape=(shape_of(4, count, width),) * 2,
        in_specs=[VMEM] * 2,
        out_specs=(VMEM,) * 2,
        cost_estimate=pl.CostEstimate(
            flops=6 * total * width * wide, bytes_accessed=8 << 20, transcendentals=0
        ),
    )
    own_part, other_part = input_call(dqkv, full)
    swapped = grid.flip(other_part, 0, 1, 0)
    pair = lambda i: own_part[i].astype(jnp.float32) + swapped[i].astype(jnp.float32)
    moves = [
        grid.flip(pair(i + 1).astype(jnp.bfloat16), db, 0, dy)
        for i, (db, dy) in enumerate(((1, 0), (0, 1), (1, 1)))
    ]
    dinput = pair(0) + sum(move.astype(jnp.float32) for move in moves)
    dinput = dinput.astype(jnp.bfloat16)

    grads = pl.pallas_call(
        functools.partial(spread_kernel, dim),
        compiler_params=room(12),
        out_shape=shape_of(shard, 4 * width, dtype=jnp.float32),
        grid=(4,),
        in_specs=[SMEM] + [VMEM] * 9,
        out_specs=pl.BlockSpec((shard, width), lambda i: (0, (i + 3) % 4)),
        scratch_shapes=[pltpu.VMEM((8, shard, 3 * wide), jnp.bfloat16)],
    )(at, *square, kept)
    if grid.groups > 1:
        same = [[2 * g + y for g in range(grid.groups)] for y in range(2)]
        grads = lax.psum(grads, "rep", axis_index_groups=same)
    return dinput.reshape(tokens.shape), grads


def solution(mesh):
    pix, rep = mesh.shape["pix"], mesh.shape["rep"]
    sites = P(BOTH, None, None)
    rows = P("pix", None)

    def step(*operands):
        return local(pix, rep, *operands)

    return jax.shard_map(
        step,
        mesh=mesh,
        in_specs=(sites, sites, rows, rows, rows, rows),
        out_specs=(sites, rows),
        check_vma=False,
    )
```

```python
import functools

import jax
import jax.numpy as jnp
from jax import lax
from jax.experimental import pallas as pl
from jax.experimental.pallas import tpu as pltpu
from jax.sharding import PartitionSpec as P


HEADS = 16
FRAMES = 16
KEPT = 2
BLOCK = 256
BOTH = ("pix", "rep")
VMEM = pl.BlockSpec(memory_space=pltpu.VMEM)
SMEM = pl.BlockSpec(memory_space=pltpu.SMEM)


def room(mib):
    return pltpu.CompilerParams(vmem_limit_bytes=mib << 20)


def matmul(left, right, dims):
    return lax.dot_general(left, right, (dims, ((), ())), preferred_element_type=jnp.float32)


def shape_of(*dims, dtype=jnp.bfloat16):
    return jax.ShapeDtypeStruct(dims, dtype)


class Grid:
    def __init__(self, pix, rep):
        self.lines, self.groups, self.rep = pix // 4, rep // 2, rep

    def all(self):
        for a in range(self.lines):
            for b in range(2):
                for c in range(2):
                    for g in range(self.groups):
                        for y in range(2):
                            yield a, b, c, g, y

    def flat(self, a, b, c, g, y):
        return (4 * a + 2 * b + c) * self.rep + 2 * g + y

    def send(self, value, target):
        pairs = []
        for source in self.all():
            to = target(*source)
            if to is not None:
                pairs.append((self.flat(*source), self.flat(*to)))
        return lax.ppermute(value, BOTH, pairs)

    def flip(self, value, db, dc, dy):
        return self.send(value, lambda a, b, c, g, y: (a, b ^ db, c ^ dc, g, y ^ dy))

    def shift(self, value, step):
        return self.send(value, lambda a, b, c, g, y: ((a + step) % self.lines, b, c, g, y))

    def gather_lines(self, value):
        lines = self.lines
        found = {0: value}
        for s in range(1, lines):
            if lines == 2 or 1 < s < lines - 1:
                found[s] = self.shift(value, s)
        if lines > 2:
            last = lines - 1
            step = lambda by: (
                lambda a, b, c, g, y: (a + by, b, c, g, y) if 0 <= a + by < lines else None
            )
            up = self.send(value, step(1))
            down = self.send(value, step(-1))
            if lines == 4:
                ends = self.send(
                    found[2],
                    lambda a, b, c, g, y: (
                        (3, b, c, g, y) if a == 2 else (0, b, c, g, y) if a == 1 else None
                    ),
                )
            else:
                ends = self.send(
                    value, lambda a, b, c, g, y: (last - a, b, c, g, y) if a in (0, last) else None
                )
            found[1], found[last], found[lines] = up, down, ends
        return [found[s] for s in range(len(found))]

    def scatter_lines(self, values):
        lines = self.lines
        if lines != 4:
            return [values[0]] + [self.shift(values[s], s) for s in range(1, lines)]

        def way(hops):
            return lambda a, b, c, g, y: (hops[a], b, c, g, y) if a in hops else None

        relay = self.send(values[4], way({0: 1, 3: 2}))
        terms = [
            values[0],
            self.send(values[2], way({0: 2, 3: 1})),
            self.send(values[1], way({0: 1, 1: 2, 2: 3})),
            self.send(values[3], way({1: 0, 2: 1, 3: 2})),
        ]
        both = values[2].astype(jnp.float32) + relay.astype(jnp.float32)
        return terms + [self.send(both.astype(jnp.bfloat16), way({1: 3, 2: 0}))]


def pack_kernel(dim, at_ref, *refs):
    sources, outs, weights, sems = refs[:3], refs[3:7], refs[7:10], refs[10]
    copies = [pltpu.make_async_copy(sources[w], weights[w], sems.at[w]) for w in range(3)]
    for copy in copies:
        copy.start()
    for copy in copies:
        copy.wait()
    even, b_here, c_here = at_ref[3] == 0, at_ref[1], at_ref[2]
    values = [ref[...] for ref in weights]
    for b in range(2):
        for c in range(2):
            pieces = []
            for value in values:
                for k in range(KEPT):
                    low = (8 * c + 4 * k + 2 * b) * dim
                    first, second = value[:, low : low + dim], value[:, low + dim : low + 2 * dim]
                    pieces.append(jnp.where(even, first, second))
            block = jnp.concatenate(pieces, axis=1)
            for db in range(2):
                for dc in range(2):

                    @pl.when((b_here == b ^ db) & (c_here == c ^ dc))
                    def _(db=db, dc=dc):
                        outs[2 * db + dc][...] = block


def plane_kernel(at_ref, *refs):
    *pieces, out_ref = refs
    here = 2 * at_ref[1] + at_ref[2]
    wide = pieces[0].shape[1]
    for n, piece in enumerate(pieces):
        index = here ^ n
        for side in range(2):

            @pl.when(index % 2 == side)
            def _(side=side, piece=piece, index=index):
                out_ref[index // 2, :, side * wide : (side + 1) * wide] = piece[...]


def sum_kernel(terms, at_ref, *refs):
    parts, heads, outs = refs[:terms], refs[terms : len(refs) - 6], refs[len(refs) - 6 :]
    here = 2 * at_ref[1] + at_ref[2]
    wide = outs[0].shape[1]
    for n, out in enumerate(outs[:4]):
        index = here ^ n
        for side in range(2):

            @pl.when(index % 2 == side)
            def _(side=side, out=out, index=index):
                cut = slice(side * wide, (side + 1) * wide)
                total = sum(p[index // 2, :, cut].astype(jnp.float32) for p in parts)
                out[...] = total.astype(jnp.bfloat16)

    kept, other = outs[4:]
    kept[...] = sum(h[...].astype(jnp.float32) for h in heads).astype(kept.dtype)
    width = kept.shape[1]
    other[:, :width] = kept[...]
    other[:, width:] = outs[0][...]


def attend(query, keyed, valued, dattn, scale, bias):
    scores = matmul(query, keyed, ((1,), (1,))) * scale + bias
    expo = jnp.exp(scores - jnp.max(scores, axis=1, keepdims=True))
    probs = expo * (1.0 / jnp.sum(expo, axis=1, keepdims=True))
    probs_b = probs.astype(jnp.bfloat16)
    attended = matmul(probs_b, valued, ((1,), (0,)))
    dvalue = matmul(probs_b, dattn, ((0,), (0,)))
    dprobs = matmul(dattn, valued, ((1,), (1,)))
    inner = jnp.sum(dprobs * probs, axis=1, keepdims=True)
    dscore = (probs * (dprobs - inner) * scale).astype(jnp.bfloat16)
    dquery = matmul(dscore, keyed, ((1,), (0,)))
    dkey = matmul(dscore, query, ((0,), (0,)))
    return [v.astype(jnp.bfloat16) for v in (attended, dquery, dkey, dvalue)]


def full_weights(lines, at_ref, planes, loose, full):
    def store(plane, line):
        for n in range(4):
            side = (n % 2) * loose.shape[2]
            loose[4 * line + n] = plane[n // 2, :, side : side + loose.shape[2]]

    last = lines - 1
    for s in range(lines):
        line = lax.rem(at_ref[0] + lines - s, lines)
        if lines > 2 and s in (1, last):
            edge = at_ref[0] == (0 if s == 1 else last)
            pl.when(edge)(functools.partial(store, planes[lines], line))
            pl.when(jnp.logical_not(edge))(functools.partial(store, planes[s], line))
        else:
            store(planes[s], line)
    shard = loose.shape[1]
    for p in range(4 * lines):
        full[p * shard : (p + 1) * shard, :] = loose[p]


def project_kernel(lines, at_ref, *refs):
    xs, xc = refs[:2]
    planes, (qkv_ref, full, loose) = refs[2:-3], refs[-3:]
    full_weights(lines, at_ref, planes, loose, full)
    half = xs.shape[0] * xs.shape[1]
    each = BLOCK // xs.shape[1]
    for part, x_ref in enumerate((xs, xc)):
        for j in range(half // BLOCK):
            x = x_ref[each * j : each * (j + 1)].reshape(BLOCK, xs.shape[-1])
            row = part * half + j * BLOCK
            value = matmul(x, full[...], ((1,), (0,)))
            qkv_ref[row : row + BLOCK, :] = value.astype(jnp.bfloat16)


def attention_kernel(scale, lines, owed, at_ref, *refs):
    xs, xc, ds, dc, qkv_ref = refs[:5]
    sent = lines + (lines == 4)
    out_ws, grads_in = refs[5 : 5 + owed], refs[5 + owed : 5 + owed + sent]
    grads_out = refs[5 + owed + sent : 5 + 2 * owed + sent]
    dqkv_ref, loose, out_w, att, grads, bias = refs[5 + 2 * owed + sent :]
    shard, wide = loose.shape[1:]
    dim = wide // (3 * KEPT)
    width = xs.shape[-1]
    if owed == 1:
        out_w[...] = out_ws[0][...]
    else:
        for s, held in enumerate(out_ws):
            line = lax.rem(at_ref[0] + lines - s, lines)
            for k in range(KEPT):

                @pl.when(line == KEPT * at_ref[2] + k)
                def _(k=k, held=held):
                    out_w[k * dim : (k + 1) * dim, :] = held[...]

    site = lambda axis: lax.broadcasted_iota(jnp.int32, (BLOCK, BLOCK), axis) // FRAMES
    bias[...] = jnp.where(site(0) == site(1), 0.0, -1e30)
    half = xs.shape[0] * xs.shape[1]
    each = BLOCK // xs.shape[1]
    for part, d_ref in enumerate((ds, dc)):

        def block(j, _, part=part, d_ref=d_ref):
            d = d_ref[pl.ds(each * j, each)].reshape(BLOCK, width)
            da = matmul(d, out_w[...], ((1,), (1,))).astype(jnp.bfloat16)
            row = pl.multiple_of(part * half + j * BLOCK, BLOCK)
            qkv = qkv_ref[pl.ds(row, BLOCK), :]
            cut = lambda v, n: v[:, n * dim : (n + 1) * dim]
            outs = [
                attend(
                    cut(qkv, k),
                    cut(qkv, KEPT + k),
                    cut(qkv, 2 * KEPT + k),
                    cut(da, k),
                    scale,
                    bias[...],
                )
                for k in range(KEPT)
            ]
            att[pl.ds(row, BLOCK), :] = jnp.concatenate([o[0] for o in outs], axis=1)
            dqkv_ref[pl.ds(row, BLOCK), :] = jnp.concatenate(
                [outs[k][n] for n in (1, 2, 3) for k in range(KEPT)], axis=1
            )
            return 0

        lax.fori_loop(0, half // BLOCK, block, 0, unroll=True)

    def columns(m, _):
        at = pl.multiple_of(m * 128, 128)
        first = matmul(att[:half, :], ds[:, :, pl.ds(at, 128)].reshape(half, 128), ((0,), (0,)))
        second = matmul(att[half:, :], dc[:, :, pl.ds(at, 128)].reshape(half, 128), ((0,), (0,)))
        term = (first + second).astype(jnp.bfloat16)
        if owed == 1:
            grads_out[0][:, pl.ds(at, 128)] = term
        for s in range(owed if owed > 1 else 0):
            upper = lax.rem(at_ref[0] + s, lines) != KEPT * at_ref[2]
            grads_out[s][:, pl.ds(at, 128)] = jnp.where(upper, term[dim:], term[:dim])
        first = matmul(xs[:, :, pl.ds(at, 128)].reshape(half, 128), dqkv_ref[:half, :], ((0,), (0,)))
        second = matmul(xc[:, :, pl.ds(at, 128)].reshape(half, 128), dqkv_ref[half:, :], ((0,), (0,)))
        grads[pl.ds(at, 128), :] = first + second
        return 0

    lax.fori_loop(0, width // 128, columns, 0, unroll=True)
    for p in range(4 * lines):
        loose[p] = grads[p * shard : (p + 1) * shard, :].astype(jnp.bfloat16)
    for s, out in enumerate(grads_in):
        line = lax.rem(at_ref[0] + s, lines)
        if s == lines:
            line = jnp.where(at_ref[0] == 0, lines - 1, 0)
        for n in range(4):
            out[n // 2, :, (n % 2) * wide : (n % 2 + 1) * wide] = loose[4 * line + n]


def input_kernel(dqkv_ref, full, own_ref, other_ref):
    chunks, count, width = own_ref.shape
    each = BLOCK // count
    for part, out in enumerate((own_ref, other_ref)):

        def block(j, _, part=part, out=out):
            row = pl.multiple_of((part * chunks + each * j) * count, BLOCK)
            value = matmul(dqkv_ref[pl.ds(row, BLOCK), :], full[...], ((1,), (1,)))
            out[pl.ds(each * j, each)] = value.astype(jnp.bfloat16).reshape(each, count, width)
            return 0

        lax.fori_loop(0, chunks // each, block, 0, unroll=True)


def spread_kernel(dim, at_ref, *refs):
    *pieces, kept_ref, out_ref, table = refs
    step = pl.program_id(0)

    @pl.when(step == 0)
    def _():
        for n, piece in enumerate(pieces):
            db, dc, dy = n // 4, (n // 2) % 2, n % 2
            b = lax.rem(at_ref[1] + db, 2)
            c = lax.rem(at_ref[2] + dc, 2)
            y = lax.rem(at_ref[3] + dy, 2)
            table[4 * b + 2 * c + y] = piece[:, piece.shape[1] - table.shape[2] :]
        moved = pieces[1][:, : out_ref.shape[1]].astype(jnp.float32)
        out_ref[...] = kept_ref[...].astype(jnp.float32) + moved

    for w in range(3):

        @pl.when(step == w + 1)
        def _(w=w):
            heads = []
            for h in range(HEADS):
                c, k, b, y = h // 8, (h // 4) % 2, (h // 2) % 2, h % 2
                low = (w * KEPT + k) * dim
                heads.append(table[4 * b + 2 * c + y, :, low : low + dim].astype(jnp.float32))
            out_ref[...] = jnp.concatenate(heads, axis=1)


def local(pix, rep, tokens, out_grad, query_weight, key_weight, value_weight, output_weight):
    grid = Grid(pix, rep)
    lines = grid.lines
    width = tokens.shape[-1]
    dim = width // HEADS
    wide = KEPT * dim
    shard = query_weight.shape[0]
    scale = 1.0 / dim**0.5
    place, rank = lax.axis_index("pix"), lax.axis_index("rep")
    a, b, c, y = place // 4, (place // 2) % 2, place % 2, rank % 2
    at = jnp.stack([a, b, c, y]).astype(jnp.int32)
    rows = tokens.reshape(-1, width)
    drows = out_grad.reshape(-1, width)
    count = rows.shape[0]
    total = 8 * count

    def gather_rows(own):
        ways = ((1, 0), (0, 1), (1, 1))
        chips = jnp.stack([own] + [grid.flip(own, db, 0, dy) for db, dy in ways])
        return chips, grid.flip(chips, 0, 1, 0)

    pieces = pl.pallas_call(
        functools.partial(pack_kernel, dim),
        compiler_params=room(8),
        out_shape=(shape_of(shard, 3 * wide),) * 4,
        in_specs=[SMEM] + [pl.BlockSpec(memory_space=pltpu.HBM)] * 3,
        out_specs=(VMEM,) * 4,
        scratch_shapes=[pltpu.VMEM((shard, width), jnp.bfloat16)] * 3
        + [pltpu.SemaphoreType.DMA((3,))],
    )(at, *[pltpu.with_memory_space_constraint(v, pltpu.HBM) for v in (query_weight, key_weight, value_weight)])
    pieces = [pieces[0]] + [grid.flip(pieces[n], n // 2, n % 2, 0) for n in range(1, 4)]
    plane = pl.pallas_call(
        plane_kernel,
        compiler_params=room(8),
        out_shape=shape_of(2, shard, 6 * wide),
        in_specs=[SMEM] + [VMEM] * 4,
        out_specs=VMEM,
    )(at, *pieces)
    xs, xc = gather_rows(rows)
    planes = grid.gather_lines(plane)

    one_head = shard == dim
    span = lines // 2
    if one_head:
        out_ws = [
            grid.send(
                output_weight,
                lambda a, b, c, g, y: (((a + s) % lines, b, a // span, g, y) if c == y else None),
            )
            for s in range(lines)
        ]
    else:
        everything = lax.all_gather(output_weight, "pix", axis=0, tiled=True)
        everything = everything.reshape(2, KEPT, 2, 2, dim, width)
        out_w = lax.dynamic_index_in_dim(everything, c, 0, keepdims=False)
        out_w = lax.dynamic_index_in_dim(
            out_w.reshape(KEPT, 4, dim, width), 2 * b + y, 1, keepdims=False
        ).reshape(wide, width)
        out_ws = [out_w]
    ds, dc = gather_rows(drows)

    sent = lines + (lines == 4)
    owed = len(out_ws)
    head_rows = dim if one_head else wide
    project = pl.pallas_call(
        functools.partial(project_kernel, lines),
        compiler_params=room(16),
        out_shape=(shape_of(total, 3 * wide), shape_of(width, 3 * wide)),
        in_specs=[SMEM] + [VMEM] * (2 + len(planes)),
        out_specs=(VMEM,) * 2,
        scratch_shapes=[pltpu.VMEM((pix, shard, 3 * wide), jnp.bfloat16)],
        cost_estimate=pl.CostEstimate(
            flops=6 * total * width * wide, bytes_accessed=6 << 20, transcendentals=0
        ),
    )
    qkv, full = project(at, xs, xc, *planes)
    *results, dqkv = pl.pallas_call(
        functools.partial(attention_kernel, scale, lines, owed),
        compiler_params=room(28),
        out_shape=(shape_of(2, shard, 6 * wide),) * sent
        + (shape_of(head_rows, width),) * owed
        + (shape_of(total, 3 * wide),),
        in_specs=[SMEM] + [VMEM] * (5 + owed),
        out_specs=(VMEM,) * (sent + owed + 1),
        scratch_shapes=[
            pltpu.VMEM((pix, shard, 3 * wide), jnp.bfloat16),
            pltpu.VMEM((wide, width), jnp.bfloat16),
            pltpu.VMEM((total, wide), jnp.bfloat16),
            pltpu.VMEM((width, 3 * wide), jnp.float32),
            pltpu.VMEM((BLOCK, BLOCK), jnp.float32),
        ],
        cost_estimate=pl.CostEstimate(
            flops=12 * total * width * wide, bytes_accessed=10 << 20, transcendentals=total * 512
        ),
    )(at, xs, xc, ds, dc, qkv, *out_ws)

    grads_in, grads_out = results[:sent], results[sent:]
    parts = grid.scatter_lines(grads_in)
    if one_head:
        heads = [
            grid.send(
                grads_out[s],
                lambda a, b, c, g, y: (
                    ((a + s) % lines, b, y, g, y) if ((a + s) % lines) // span == c else None
                ),
            )
            for s in range(lines)
        ]
    else:
        whole = jnp.zeros((2, KEPT, 2, 2, dim, width), jnp.float32)
        whole = lax.dynamic_update_slice(
            whole,
            grads_out[0].astype(jnp.float32).reshape(1, KEPT, 1, 1, dim, width),
            (c, 0, b, y, 0, 0),
        ).reshape(width, width)
        heads = [lax.psum_scatter(whole, "pix", scatter_dimension=0, tiled=True)]
    *summed, kept, other = pl.pallas_call(
        functools.partial(sum_kernel, len(parts)),
        compiler_params=room(10),
        out_shape=(shape_of(shard, 3 * wide),) * 4
        + (shape_of(shard, width), shape_of(shard, width + 3 * wide)),
        in_specs=[SMEM] + [VMEM] * (len(parts) + len(heads)),
        out_specs=(VMEM,) * 6,
    )(at, *parts, *heads)
    square = []
    for n in range(8):
        block = other if n == 1 else summed[n // 2]
        square.append(grid.flip(block, n // 4, (n // 2) % 2, n % 2) if n else block)

    input_call = pl.pallas_call(
        input_kernel,
        compiler_params=room(20),
        out_shape=(shape_of(4, count, width),) * 2,
        in_specs=[VMEM] * 2,
        out_specs=(VMEM,) * 2,
        cost_estimate=pl.CostEstimate(
            flops=6 * total * width * wide, bytes_accessed=8 << 20, transcendentals=0
        ),
    )
    own_part, other_part = input_call(dqkv, full)
    swapped = grid.flip(other_part, 0, 1, 0)
    pair = lambda i: own_part[i].astype(jnp.float32) + swapped[i].astype(jnp.float32)
    moves = [
        grid.flip(pair(i + 1).astype(jnp.bfloat16), db, 0, dy)
        for i, (db, dy) in enumerate(((1, 0), (0, 1), (1, 1)))
    ]
    dinput = pair(0) + sum(move.astype(jnp.float32) for move in moves)
    dinput = dinput.astype(jnp.bfloat16)

    grads = pl.pallas_call(
        functools.partial(spread_kernel, dim),
        compiler_params=room(12),
        out_shape=shape_of(shard, 4 * width, dtype=jnp.float32),
        grid=(4,),
        in_specs=[SMEM] + [VMEM] * 9,
        out_specs=pl.BlockSpec((shard, width), lambda i: (0, (i + 3) % 4)),
        scratch_shapes=[pltpu.VMEM((8, shard, 3 * wide), jnp.bfloat16)],
    )(at, *square, kept)
    if grid.groups > 1:
        same = [[2 * g + y for g in range(grid.groups)] for y in range(2)]
        grads = lax.psum(grads, "rep", axis_index_groups=same)
    return dinput.reshape(tokens.shape), grads


def solution(mesh):
    pix, rep = mesh.shape["pix"], mesh.shape["rep"]
    sites = P(BOTH, None, None)
    rows = P("pix", None)

    def step(*operands):
        return local(pix, rep, *operands)

    return jax.shard_map(
        step,
        mesh=mesh,
        in_specs=(sites, sites, rows, rows, rows, rows),
        out_specs=(sites, rows),
        check_vma=False,
    )
```

```python
import functools

import jax
import jax.numpy as jnp
from jax import lax
from jax.experimental import pallas as pl
from jax.experimental.pallas import tpu as pltpu
from jax.sharding import PartitionSpec as P


HEADS = 16
FRAMES = 16
KEPT = 2
BLOCK = 256
BOTH = ("pix", "rep")
VMEM = pl.BlockSpec(memory_space=pltpu.VMEM)
SMEM = pl.BlockSpec(memory_space=pltpu.SMEM)


def room(mib):
    return pltpu.CompilerParams(vmem_limit_bytes=mib << 20)


def matmul(left, right, dims):
    return lax.dot_general(left, right, (dims, ((), ())), preferred_element_type=jnp.float32)


def shape_of(*dims, dtype=jnp.bfloat16):
    return jax.ShapeDtypeStruct(dims, dtype)


class Grid:
    def __init__(self, pix, rep):
        self.lines, self.groups, self.rep = pix // 4, rep // 2, rep

    def all(self):
        for a in range(self.lines):
            for b in range(2):
                for c in range(2):
                    for g in range(self.groups):
                        for y in range(2):
                            yield a, b, c, g, y

    def flat(self, a, b, c, g, y):
        return (4 * a + 2 * b + c) * self.rep + 2 * g + y

    def send(self, value, target):
        pairs = []
        for source in self.all():
            to = target(*source)
            if to is not None:
                pairs.append((self.flat(*source), self.flat(*to)))
        return lax.ppermute(value, BOTH, pairs)

    def flip(self, value, db, dc, dy):
        return self.send(value, lambda a, b, c, g, y: (a, b ^ db, c ^ dc, g, y ^ dy))

    def shift(self, value, step):
        return self.send(value, lambda a, b, c, g, y: ((a + step) % self.lines, b, c, g, y))

    def gather_lines(self, value):
        lines = self.lines
        found = {0: value}
        for s in range(1, lines):
            if lines == 2 or 1 < s < lines - 1:
                found[s] = self.shift(value, s)
        if lines > 2:
            last = lines - 1
            step = lambda by: (
                lambda a, b, c, g, y: (a + by, b, c, g, y) if 0 <= a + by < lines else None
            )
            up = self.send(value, step(1))
            down = self.send(value, step(-1))
            if lines == 4:
                ends = self.send(
                    found[2],
                    lambda a, b, c, g, y: (
                        (3, b, c, g, y) if a == 2 else (0, b, c, g, y) if a == 1 else None
                    ),
                )
            else:
                ends = self.send(
                    value, lambda a, b, c, g, y: (last - a, b, c, g, y) if a in (0, last) else None
                )
            found[1], found[last], found[lines] = up, down, ends
        return [found[s] for s in range(len(found))]

    def scatter_lines(self, values):
        lines = self.lines
        if lines != 4:
            return [values[0]] + [self.shift(values[s], s) for s in range(1, lines)]

        def way(hops):
            return lambda a, b, c, g, y: (hops[a], b, c, g, y) if a in hops else None

        relay = self.send(values[4], way({0: 1, 3: 2}))
        terms = [
            values[0],
            self.send(values[2], way({0: 2, 3: 1})),
            self.send(values[1], way({0: 1, 1: 2, 2: 3})),
            self.send(values[3], way({1: 0, 2: 1, 3: 2})),
        ]
        both = values[2].astype(jnp.float32) + relay.astype(jnp.float32)
        return terms + [self.send(both.astype(jnp.bfloat16), way({1: 3, 2: 0}))]


def pack_kernel(dim, at_ref, *refs):
    sources, outs, weights, sems = refs[:3], refs[3:7], refs[7:10], refs[10]
    copies = [pltpu.make_async_copy(sources[w], weights[w], sems.at[w]) for w in range(3)]
    for copy in copies:
        copy.start()
    for copy in copies:
        copy.wait()
    even, b_here, c_here = at_ref[3] == 0, at_ref[1], at_ref[2]
    values = [ref[...] for ref in weights]
    for b in range(2):
        for c in range(2):
            pieces = []
            for value in values:
                for k in range(KEPT):
                    low = (8 * c + 4 * k + 2 * b) * dim
                    first, second = value[:, low : low + dim], value[:, low + dim : low + 2 * dim]
                    pieces.append(jnp.where(even, first, second))
            block = jnp.concatenate(pieces, axis=1)
            for db in range(2):
                for dc in range(2):

                    @pl.when((b_here == b ^ db) & (c_here == c ^ dc))
                    def _(db=db, dc=dc):
                        outs[2 * db + dc][...] = block


def plane_kernel(at_ref, *refs):
    *pieces, out_ref = refs
    here = 2 * at_ref[1] + at_ref[2]
    wide = pieces[0].shape[1]
    for n, piece in enumerate(pieces):
        index = here ^ n
        for side in range(2):

            @pl.when(index % 2 == side)
            def _(side=side, piece=piece, index=index):
                out_ref[index // 2, :, side * wide : (side + 1) * wide] = piece[...]


def sum_kernel(at_ref, *refs):
    parts, outs = refs[: len(refs) - 4], refs[len(refs) - 4 :]
    here = 2 * at_ref[1] + at_ref[2]
    wide = outs[0].shape[1]
    for n, out in enumerate(outs):
        index = here ^ n
        for side in range(2):

            @pl.when(index % 2 == side)
            def _(side=side, out=out, index=index):
                cut = slice(side * wide, (side + 1) * wide)
                total = sum(p[index // 2, :, cut].astype(jnp.float32) for p in parts)
                out[...] = total.astype(jnp.bfloat16)


def attend(query, keyed, valued, dattn, scale, bias):
    scores = matmul(query, keyed, ((1,), (1,))) * scale + bias
    expo = jnp.exp(scores - jnp.max(scores, axis=1, keepdims=True))
    probs = expo * (1.0 / jnp.sum(expo, axis=1, keepdims=True))
    probs_b = probs.astype(jnp.bfloat16)
    attended = matmul(probs_b, valued, ((1,), (0,)))
    dvalue = matmul(probs_b, dattn, ((0,), (0,)))
    dprobs = matmul(dattn, valued, ((1,), (1,)))
    inner = jnp.sum(dprobs * probs, axis=1, keepdims=True)
    dscore = (probs * (dprobs - inner) * scale).astype(jnp.bfloat16)
    dquery = matmul(dscore, keyed, ((1,), (0,)))
    dkey = matmul(dscore, query, ((0,), (0,)))
    return [v.astype(jnp.bfloat16) for v in (attended, dquery, dkey, dvalue)]


def full_weights(lines, at_ref, planes, loose, full):
    def store(plane, line):
        for n in range(4):
            side = (n % 2) * loose.shape[2]
            loose[4 * line + n] = plane[n // 2, :, side : side + loose.shape[2]]

    last = lines - 1
    for s in range(lines):
        line = lax.rem(at_ref[0] + lines - s, lines)
        if lines > 2 and s in (1, last):
            edge = at_ref[0] == (0 if s == 1 else last)
            pl.when(edge)(functools.partial(store, planes[lines], line))
            pl.when(jnp.logical_not(edge))(functools.partial(store, planes[s], line))
        else:
            store(planes[s], line)
    shard = loose.shape[1]
    for p in range(4 * lines):
        full[p * shard : (p + 1) * shard, :] = loose[p]


def project_kernel(lines, at_ref, *refs):
    xs, xc = refs[:2]
    planes, (qkv_ref, full, loose) = refs[2:-3], refs[-3:]
    full_weights(lines, at_ref, planes, loose, full)
    half = xs.shape[0] * xs.shape[1]
    each = BLOCK // xs.shape[1]
    for part, x_ref in enumerate((xs, xc)):
        for j in range(half // BLOCK):
            x = x_ref[each * j : each * (j + 1)].reshape(BLOCK, xs.shape[-1])
            row = part * half + j * BLOCK
            value = matmul(x, full[...], ((1,), (0,)))
            qkv_ref[row : row + BLOCK, :] = value.astype(jnp.bfloat16)


def attention_kernel(scale, lines, owed, at_ref, *refs):
    ds, dc, qkv_ref = refs[:3]
    out_ws, grads_out = refs[3 : 3 + owed], refs[3 + owed : 3 + 2 * owed]
    dqkv_ref, out_w, att, bias = refs[3 + 2 * owed :]
    dim = out_w.shape[0] // KEPT
    width = ds.shape[-1]
    if owed == 1:
        out_w[...] = out_ws[0][...]
    else:
        for s, held in enumerate(out_ws):
            line = lax.rem(at_ref[0] + lines - s, lines)
            for k in range(KEPT):

                @pl.when(line == KEPT * at_ref[2] + k)
                def _(k=k, held=held):
                    out_w[k * dim : (k + 1) * dim, :] = held[...]

    site = lambda axis: lax.broadcasted_iota(jnp.int32, (BLOCK, BLOCK), axis) // FRAMES
    bias[...] = jnp.where(site(0) == site(1), 0.0, -1e30)
    half = ds.shape[0] * ds.shape[1]
    each = BLOCK // ds.shape[1]
    for part, d_ref in enumerate((ds, dc)):

        def block(j, _, part=part, d_ref=d_ref):
            d = d_ref[pl.ds(each * j, each)].reshape(BLOCK, width)
            da = matmul(d, out_w[...], ((1,), (1,))).astype(jnp.bfloat16)
            row = pl.multiple_of(part * half + j * BLOCK, BLOCK)
            qkv = qkv_ref[pl.ds(row, BLOCK), :]
            cut = lambda v, n: v[:, n * dim : (n + 1) * dim]
            outs = [
                attend(
                    cut(qkv, k),
                    cut(qkv, KEPT + k),
                    cut(qkv, 2 * KEPT + k),
                    cut(da, k),
                    scale,
                    bias[...],
                )
                for k in range(KEPT)
            ]
            att[pl.ds(row, BLOCK), :] = jnp.concatenate([o[0] for o in outs], axis=1)
            dqkv_ref[pl.ds(row, BLOCK), :] = jnp.concatenate(
                [outs[k][n] for n in (1, 2, 3) for k in range(KEPT)], axis=1
            )
            return 0

        lax.fori_loop(0, half // BLOCK, block, 0, unroll=True)

    def columns(m, _):
        at = pl.multiple_of(m * 128, 128)
        first = matmul(att[:half, :], ds[:, :, pl.ds(at, 128)].reshape(half, 128), ((0,), (0,)))
        second = matmul(att[half:, :], dc[:, :, pl.ds(at, 128)].reshape(half, 128), ((0,), (0,)))
        term = (first + second).astype(jnp.bfloat16)
        if owed == 1:
            grads_out[0][:, pl.ds(at, 128)] = term
        for s in range(owed if owed > 1 else 0):
            upper = lax.rem(at_ref[0] + s, lines) != KEPT * at_ref[2]
            grads_out[s][:, pl.ds(at, 128)] = jnp.where(upper, term[dim:], term[:dim])
        return 0

    lax.fori_loop(0, width // 128, columns, 0, unroll=True)


def weight_kernel(at_ref, xs, xc, dqkv_ref, *refs):
    grads_in, (loose, grads) = refs[:-2], refs[-2:]
    lines = loose.shape[0] // 4
    shard, wide = loose.shape[1:]
    half = xs.shape[0] * xs.shape[1]

    def columns(m, _):
        at = pl.multiple_of(m * 128, 128)
        first = matmul(xs[:, :, pl.ds(at, 128)].reshape(half, 128), dqkv_ref[:half, :], ((0,), (0,)))
        second = matmul(xc[:, :, pl.ds(at, 128)].reshape(half, 128), dqkv_ref[half:, :], ((0,), (0,)))
        grads[pl.ds(at, 128), :] = first + second
        return 0

    lax.fori_loop(0, xs.shape[-1] // 128, columns, 0, unroll=True)
    for p in range(4 * lines):
        loose[p] = grads[p * shard : (p + 1) * shard, :].astype(jnp.bfloat16)
    for s, out in enumerate(grads_in):
        line = lax.rem(at_ref[0] + s, lines)
        if s == lines:
            line = jnp.where(at_ref[0] == 0, lines - 1, 0)
        for n in range(4):
            out[n // 2, :, (n % 2) * wide : (n % 2 + 1) * wide] = loose[4 * line + n]


def input_kernel(dqkv_ref, full, own_ref, other_ref):
    chunks, count, width = own_ref.shape
    each = BLOCK // count
    for part, out in enumerate((own_ref, other_ref)):

        def block(j, _, part=part, out=out):
            row = pl.multiple_of((part * chunks + each * j) * count, BLOCK)
            value = matmul(dqkv_ref[pl.ds(row, BLOCK), :], full[...], ((1,), (1,)))
            out[pl.ds(each * j, each)] = value.astype(jnp.bfloat16).reshape(each, count, width)
            return 0

        lax.fori_loop(0, chunks // each, block, 0, unroll=True)


def spread_kernel(dim, at_ref, *refs):
    *pieces, kept_ref, moved_ref, out_ref, table = refs
    step = pl.program_id(0)

    @pl.when(step == 0)
    def _():
        for n, piece in enumerate(pieces):
            db, dc, dy = n // 4, (n // 2) % 2, n % 2
            b = lax.rem(at_ref[1] + db, 2)
            c = lax.rem(at_ref[2] + dc, 2)
            y = lax.rem(at_ref[3] + dy, 2)
            table[4 * b + 2 * c + y] = piece[...]
        out_ref[...] = kept_ref[...].astype(jnp.float32) + moved_ref[...].astype(jnp.float32)

    for w in range(3):

        @pl.when(step == w + 1)
        def _(w=w):
            heads = []
            for h in range(HEADS):
                c, k, b, y = h // 8, (h // 4) % 2, (h // 2) % 2, h % 2
                low = (w * KEPT + k) * dim
                heads.append(table[4 * b + 2 * c + y, :, low : low + dim].astype(jnp.float32))
            out_ref[...] = jnp.concatenate(heads, axis=1)


def local(pix, rep, tokens, out_grad, query_weight, key_weight, value_weight, output_weight):
    grid = Grid(pix, rep)
    lines = grid.lines
    width = tokens.shape[-1]
    dim = width // HEADS
    wide = KEPT * dim
    shard = query_weight.shape[0]
    scale = 1.0 / dim**0.5
    place, rank = lax.axis_index("pix"), lax.axis_index("rep")
    a, b, c, y = place // 4, (place // 2) % 2, place % 2, rank % 2
    at = jnp.stack([a, b, c, y]).astype(jnp.int32)
    rows = tokens.reshape(-1, width)
    drows = out_grad.reshape(-1, width)
    count = rows.shape[0]
    total = 8 * count

    def gather_rows(own):
        ways = ((1, 0), (0, 1), (1, 1))
        chips = jnp.stack([own] + [grid.flip(own, db, 0, dy) for db, dy in ways])
        return chips, grid.flip(chips, 0, 1, 0)

    pieces = pl.pallas_call(
        functools.partial(pack_kernel, dim),
        compiler_params=room(8),
        out_shape=(shape_of(shard, 3 * wide),) * 4,
        in_specs=[SMEM] + [pl.BlockSpec(memory_space=pltpu.HBM)] * 3,
        out_specs=(VMEM,) * 4,
        scratch_shapes=[pltpu.VMEM((shard, width), jnp.bfloat16)] * 3
        + [pltpu.SemaphoreType.DMA((3,))],
    )(at, *[pltpu.with_memory_space_constraint(v, pltpu.HBM) for v in (query_weight, key_weight, value_weight)])
    pieces = [pieces[0]] + [grid.flip(pieces[n], n // 2, n % 2, 0) for n in range(1, 4)]
    plane = pl.pallas_call(
        plane_kernel,
        compiler_params=room(8),
        out_shape=shape_of(2, shard, 6 * wide),
        in_specs=[SMEM] + [VMEM] * 4,
        out_specs=VMEM,
    )(at, *pieces)
    xs, xc = gather_rows(rows)
    planes = grid.gather_lines(plane)

    one_head = shard == dim
    span = lines // 2
    if one_head:
        out_ws = [
            grid.send(
                output_weight,
                lambda a, b, c, g, y: (((a + s) % lines, b, a // span, g, y) if c == y else None),
            )
            for s in range(lines)
        ]
    else:
        everything = lax.all_gather(output_weight, "pix", axis=0, tiled=True)
        everything = everything.reshape(2, KEPT, 2, 2, dim, width)
        out_w = lax.dynamic_index_in_dim(everything, c, 0, keepdims=False)
        out_w = lax.dynamic_index_in_dim(
            out_w.reshape(KEPT, 4, dim, width), 2 * b + y, 1, keepdims=False
        ).reshape(wide, width)
        out_ws = [out_w]
    ds, dc = gather_rows(drows)

    sent = lines + (lines == 4)
    owed = len(out_ws)
    head_rows = dim if one_head else wide
    project = pl.pallas_call(
        functools.partial(project_kernel, lines),
        compiler_params=room(16),
        out_shape=(shape_of(total, 3 * wide), shape_of(width, 3 * wide)),
        in_specs=[SMEM] + [VMEM] * (2 + len(planes)),
        out_specs=(VMEM,) * 2,
        scratch_shapes=[pltpu.VMEM((pix, shard, 3 * wide), jnp.bfloat16)],
        cost_estimate=pl.CostEstimate(
            flops=6 * total * width * wide, bytes_accessed=6 << 20, transcendentals=0
        ),
    )
    qkv, full = project(at, xs, xc, *planes)
    *grads_out, dqkv = pl.pallas_call(
        functools.partial(attention_kernel, scale, lines, owed),
        compiler_params=room(24),
        out_shape=(shape_of(head_rows, width),) * owed + (shape_of(total, 3 * wide),),
        in_specs=[SMEM] + [VMEM] * (3 + owed),
        out_specs=(VMEM,) * (owed + 1),
        scratch_shapes=[
            pltpu.VMEM((wide, width), jnp.bfloat16),
            pltpu.VMEM((total, wide), jnp.bfloat16),
            pltpu.VMEM((BLOCK, BLOCK), jnp.float32),
        ],
        cost_estimate=pl.CostEstimate(
            flops=6 * total * width * wide, bytes_accessed=6 << 20, transcendentals=total * 512
        ),
    )(at, ds, dc, qkv, *out_ws)
    weigh = pl.pallas_call(
        weight_kernel,
        compiler_params=room(20),
        out_shape=(shape_of(2, shard, 6 * wide),) * sent,
        in_specs=[SMEM] + [VMEM] * 3,
        out_specs=(VMEM,) * sent,
        scratch_shapes=[
            pltpu.VMEM((pix, shard, 3 * wide), jnp.bfloat16),
            pltpu.VMEM((width, 3 * wide), jnp.float32),
        ],
        cost_estimate=pl.CostEstimate(
            flops=6 * total * width * wide, bytes_accessed=5 << 20, transcendentals=0
        ),
    )
    grads_in = weigh(at, xs, xc, dqkv)

    parts = grid.scatter_lines(grads_in)
    if one_head:
        heads = [
            grid.send(
                grads_out[s],
                lambda a, b, c, g, y: (
                    ((a + s) % lines, b, y, g, y) if ((a + s) % lines) // span == c else None
                ),
            )
            for s in range(lines)
        ]
    else:
        whole = jnp.zeros((2, KEPT, 2, 2, dim, width), jnp.float32)
        whole = lax.dynamic_update_slice(
            whole,
            grads_out[0].astype(jnp.float32).reshape(1, KEPT, 1, 1, dim, width),
            (c, 0, b, y, 0, 0),
        ).reshape(width, width)
        heads = [lax.psum_scatter(whole, "pix", scatter_dimension=0, tiled=True)]
    kept = sum(head.astype(jnp.float32) for head in heads).astype(jnp.bfloat16)
    if one_head:
        moved = grid.send(kept, lambda a, b, c, g, y: (a, b, c, g, y ^ 1) if c == y else None)
    else:
        moved = grid.flip(kept, 0, 0, 1)
    summed = pl.pallas_call(
        sum_kernel,
        compiler_params=room(8),
        out_shape=(shape_of(shard, 3 * wide),) * 4,
        in_specs=[SMEM] + [VMEM] * len(parts),
        out_specs=(VMEM,) * 4,
    )(at, *parts)
    square = []
    for n in range(8):
        block = summed[n // 2]
        square.append(grid.flip(block, n // 4, (n // 2) % 2, n % 2) if n else block)

    input_call = pl.pallas_call(
        input_kernel,
        compiler_params=room(20),
        out_shape=(shape_of(4, count, width),) * 2,
        in_specs=[VMEM] * 2,
        out_specs=(VMEM,) * 2,
        cost_estimate=pl.CostEstimate(
            flops=6 * total * width * wide, bytes_accessed=8 << 20, transcendentals=0
        ),
    )
    own_part, other_part = input_call(dqkv, full)
    swapped = grid.flip(other_part, 0, 1, 0)
    pair = lambda i: own_part[i].astype(jnp.float32) + swapped[i].astype(jnp.float32)
    moves = [
        grid.flip(pair(i + 1).astype(jnp.bfloat16), db, 0, dy)
        for i, (db, dy) in enumerate(((1, 0), (0, 1), (1, 1)))
    ]
    dinput = pair(0) + sum(move.astype(jnp.float32) for move in moves)
    dinput = dinput.astype(jnp.bfloat16)

    grads = pl.pallas_call(
        functools.partial(spread_kernel, dim),
        compiler_params=room(12),
        out_shape=shape_of(shard, 4 * width, dtype=jnp.float32),
        grid=(4,),
        in_specs=[SMEM] + [VMEM] * 10,
        out_specs=pl.BlockSpec((shard, width), lambda i: (0, (i + 3) % 4)),
        scratch_shapes=[pltpu.VMEM((8, shard, 3 * wide), jnp.bfloat16)],
    )(at, *square, kept, moved)
    if grid.groups > 1:
        same = [[2 * g + y for g in range(grid.groups)] for y in range(2)]
        grads = lax.psum(grads, "rep", axis_index_groups=same)
    return dinput.reshape(tokens.shape), grads


def solution(mesh):
    pix, rep = mesh.shape["pix"], mesh.shape["rep"]
    sites = P(BOTH, None, None)
    rows = P("pix", None)

    def step(*operands):
        return local(pix, rep, *operands)

    return jax.shard_map(
        step,
        mesh=mesh,
        in_specs=(sites, sites, rows, rows, rows, rows),
        out_specs=(sites, rows),
        check_vma=False,
    )
```

```python
import functools

import jax
import jax.numpy as jnp
from jax import lax
from jax.experimental import pallas as pl
from jax.experimental.pallas import tpu as pltpu
from jax.sharding import PartitionSpec as P


HEADS = 16
FRAMES = 16
KEPT = 2
BLOCK = 256
BOTH = ("pix", "rep")
VMEM = pl.BlockSpec(memory_space=pltpu.VMEM)
SMEM = pl.BlockSpec(memory_space=pltpu.SMEM)


def room(mib):
    return pltpu.CompilerParams(vmem_limit_bytes=mib << 20)


def matmul(left, right, dims):
    return lax.dot_general(left, right, (dims, ((), ())), preferred_element_type=jnp.float32)


def shape_of(*dims, dtype=jnp.bfloat16):
    return jax.ShapeDtypeStruct(dims, dtype)


class Grid:
    def __init__(self, pix, rep):
        self.lines, self.groups, self.rep = pix // 4, rep // 2, rep

    def all(self):
        for a in range(self.lines):
            for b in range(2):
                for c in range(2):
                    for g in range(self.groups):
                        for y in range(2):
                            yield a, b, c, g, y

    def flat(self, a, b, c, g, y):
        return (4 * a + 2 * b + c) * self.rep + 2 * g + y

    def send(self, value, target):
        pairs = []
        for source in self.all():
            to = target(*source)
            if to is not None:
                pairs.append((self.flat(*source), self.flat(*to)))
        return lax.ppermute(value, BOTH, pairs)

    def flip(self, value, db, dc, dy):
        return self.send(value, lambda a, b, c, g, y: (a, b ^ db, c ^ dc, g, y ^ dy))

    def shift(self, value, step):
        return self.send(value, lambda a, b, c, g, y: ((a + step) % self.lines, b, c, g, y))

    def gather_lines(self, value):
        lines = self.lines
        found = {0: value}
        for s in range(1, lines):
            if lines == 2 or 1 < s < lines - 1:
                found[s] = self.shift(value, s)
        if lines > 2:
            last = lines - 1
            step = lambda by: (
                lambda a, b, c, g, y: (a + by, b, c, g, y) if 0 <= a + by < lines else None
            )
            up = self.send(value, step(1))
            down = self.send(value, step(-1))
            if lines == 4:
                ends = self.send(
                    found[2],
                    lambda a, b, c, g, y: (
                        (3, b, c, g, y) if a == 2 else (0, b, c, g, y) if a == 1 else None
                    ),
                )
            else:
                ends = self.send(
                    value, lambda a, b, c, g, y: (last - a, b, c, g, y) if a in (0, last) else None
                )
            found[1], found[last], found[lines] = up, down, ends
        return [found[s] for s in range(len(found))]


def pack_kernel(dim, at_ref, *refs):
    sources, outs, weights, sems = refs[:3], refs[3:7], refs[7:10], refs[10]
    copies = [pltpu.make_async_copy(sources[w], weights[w], sems.at[w]) for w in range(3)]
    for copy in copies:
        copy.start()
    for copy in copies:
        copy.wait()
    even, b_here, c_here = at_ref[3] == 0, at_ref[1], at_ref[2]
    values = [ref[...] for ref in weights]
    for b in range(2):
        for c in range(2):
            pieces = []
            for value in values:
                for k in range(KEPT):
                    low = (8 * c + 4 * k + 2 * b) * dim
                    first, second = value[:, low : low + dim], value[:, low + dim : low + 2 * dim]
                    pieces.append(jnp.where(even, first, second))
            block = jnp.concatenate(pieces, axis=1)
            for db in range(2):
                for dc in range(2):

                    @pl.when((b_here == b ^ db) & (c_here == c ^ dc))
                    def _(db=db, dc=dc):
                        outs[2 * db + dc][...] = block


def plane_kernel(at_ref, *refs):
    *pieces, out_ref = refs
    here = 2 * at_ref[1] + at_ref[2]
    wide = pieces[0].shape[1]
    for n, piece in enumerate(pieces):
        index = here ^ n
        for side in range(2):

            @pl.when(index % 2 == side)
            def _(side=side, piece=piece, index=index):
                out_ref[index // 2, :, side * wide : (side + 1) * wide] = piece[...]


def sum_kernel(at_ref, *refs):
    parts, outs = refs[: len(refs) - 4], refs[len(refs) - 4 :]
    here = 2 * at_ref[1] + at_ref[2]
    wide = outs[0].shape[1]
    for n, out in enumerate(outs):
        index = here ^ n
        for side in range(2):

            @pl.when(index % 2 == side)
            def _(side=side, out=out, index=index):
                cut = slice(side * wide, (side + 1) * wide)
                total = sum(p[index // 2, :, cut].astype(jnp.float32) for p in parts)
                out[...] = total.astype(jnp.bfloat16)


def attend(query, keyed, valued, dattn, scale, bias):
    scores = matmul(query, keyed, ((1,), (1,))) * scale + bias
    expo = jnp.exp(scores - jnp.max(scores, axis=1, keepdims=True))
    probs = expo * (1.0 / jnp.sum(expo, axis=1, keepdims=True))
    probs_b = probs.astype(jnp.bfloat16)
    attended = matmul(probs_b, valued, ((1,), (0,)))
    dvalue = matmul(probs_b, dattn, ((0,), (0,)))
    dprobs = matmul(dattn, valued, ((1,), (1,)))
    inner = jnp.sum(dprobs * probs, axis=1, keepdims=True)
    dscore = (probs * (dprobs - inner) * scale).astype(jnp.bfloat16)
    dquery = matmul(dscore, keyed, ((1,), (0,)))
    dkey = matmul(dscore, query, ((0,), (0,)))
    return [v.astype(jnp.bfloat16) for v in (attended, dquery, dkey, dvalue)]


def full_weights(lines, at_ref, planes, loose, full):
    def store(plane, line):
        for n in range(4):
            side = (n % 2) * loose.shape[2]
            loose[4 * line + n] = plane[n // 2, :, side : side + loose.shape[2]]

    last = lines - 1
    for s in range(lines):
        line = lax.rem(at_ref[0] + lines - s, lines)
        if lines > 2 and s in (1, last):
            edge = at_ref[0] == (0 if s == 1 else last)
            pl.when(edge)(functools.partial(store, planes[lines], line))
            pl.when(jnp.logical_not(edge))(functools.partial(store, planes[s], line))
        else:
            store(planes[s], line)
    shard = loose.shape[1]
    for p in range(4 * lines):
        full[p * shard : (p + 1) * shard, :] = loose[p]


def project_kernel(lines, at_ref, *refs):
    xs, xc = refs[:2]
    planes, (qkv_ref, full, loose) = refs[2:-3], refs[-3:]
    full_weights(lines, at_ref, planes, loose, full)
    half = xs.shape[0] * xs.shape[1]
    each = BLOCK // xs.shape[1]
    for part, x_ref in enumerate((xs, xc)):
        for j in range(half // BLOCK):
            x = x_ref[each * j : each * (j + 1)].reshape(BLOCK, xs.shape[-1])
            row = part * half + j * BLOCK
            value = matmul(x, full[...], ((1,), (0,)))
            qkv_ref[row : row + BLOCK, :] = value.astype(jnp.bfloat16)


def attention_kernel(scale, lines, owed, at_ref, *refs):
    ds, dc, qkv_ref = refs[:3]
    out_ws, grads_out = refs[3 : 3 + owed], refs[3 + owed : 3 + 2 * owed]
    dqkv_ref, out_w, att, bias = refs[3 + 2 * owed :]
    dim = out_w.shape[0] // KEPT
    width = ds.shape[-1]
    if owed == 1:
        out_w[...] = out_ws[0][...]
    else:
        for s, held in enumerate(out_ws):
            line = lax.rem(at_ref[0] + lines - s, lines)
            for k in range(KEPT):

                @pl.when(line == KEPT * at_ref[2] + k)
                def _(k=k, held=held):
                    out_w[k * dim : (k + 1) * dim, :] = held[...]

    site = lambda axis: lax.broadcasted_iota(jnp.int32, (BLOCK, BLOCK), axis) // FRAMES
    bias[...] = jnp.where(site(0) == site(1), 0.0, -1e30)
    half = ds.shape[0] * ds.shape[1]
    each = BLOCK // ds.shape[1]
    for part, d_ref in enumerate((ds, dc)):

        def block(j, _, part=part, d_ref=d_ref):
            d = d_ref[pl.ds(each * j, each)].reshape(BLOCK, width)
            da = matmul(d, out_w[...], ((1,), (1,))).astype(jnp.bfloat16)
            row = pl.multiple_of(part * half + j * BLOCK, BLOCK)
            qkv = qkv_ref[pl.ds(row, BLOCK), :]
            cut = lambda v, n: v[:, n * dim : (n + 1) * dim]
            outs = [
                attend(
                    cut(qkv, k),
                    cut(qkv, KEPT + k),
                    cut(qkv, 2 * KEPT + k),
                    cut(da, k),
                    scale,
                    bias[...],
                )
                for k in range(KEPT)
            ]
            att[pl.ds(row, BLOCK), :] = jnp.concatenate([o[0] for o in outs], axis=1)
            dqkv_ref[pl.ds(row, BLOCK), :] = jnp.concatenate(
                [outs[k][n] for n in (1, 2, 3) for k in range(KEPT)], axis=1
            )
            return 0

        lax.fori_loop(0, half // BLOCK, block, 0, unroll=True)

    def columns(m, _):
        at = pl.multiple_of(m * 128, 128)
        first = matmul(att[:half, :], ds[:, :, pl.ds(at, 128)].reshape(half, 128), ((0,), (0,)))
        second = matmul(att[half:, :], dc[:, :, pl.ds(at, 128)].reshape(half, 128), ((0,), (0,)))
        term = (first + second).astype(jnp.bfloat16)
        if owed == 1:
            grads_out[0][:, pl.ds(at, 128)] = term
        for s in range(owed if owed > 1 else 0):
            upper = lax.rem(at_ref[0] + s, lines) != KEPT * at_ref[2]
            grads_out[s][:, pl.ds(at, 128)] = jnp.where(upper, term[dim:], term[:dim])
        return 0

    lax.fori_loop(0, width // 128, columns, 0, unroll=True)


def weight_kernel(at_ref, xs, xc, dqkv_ref, *refs):
    grads_in, (loose, grads) = refs[:-2], refs[-2:]
    lines = loose.shape[0] // 4
    shard, wide = loose.shape[1:]
    half = xs.shape[0] * xs.shape[1]

    def columns(m, _):
        at = pl.multiple_of(m * 128, 128)
        first = matmul(xs[:, :, pl.ds(at, 128)].reshape(half, 128), dqkv_ref[:half, :], ((0,), (0,)))
        second = matmul(xc[:, :, pl.ds(at, 128)].reshape(half, 128), dqkv_ref[half:, :], ((0,), (0,)))
        grads[pl.ds(at, 128), :] = first + second
        return 0

    lax.fori_loop(0, xs.shape[-1] // 128, columns, 0, unroll=True)
    for p in range(4 * lines):
        loose[p] = grads[p * shard : (p + 1) * shard, :].astype(jnp.bfloat16)
    for s, out in enumerate(grads_in):
        line = lax.rem(at_ref[0] + s, lines)
        for n in range(4):
            out[n // 2, :, (n % 2) * wide : (n % 2 + 1) * wide] = loose[4 * line + n]


def input_kernel(dqkv_ref, full, own_ref, other_ref):
    chunks, count, width = own_ref.shape
    each = BLOCK // count
    for part, out in enumerate((own_ref, other_ref)):

        def block(j, _, part=part, out=out):
            row = pl.multiple_of((part * chunks + each * j) * count, BLOCK)
            value = matmul(dqkv_ref[pl.ds(row, BLOCK), :], full[...], ((1,), (1,)))
            out[pl.ds(each * j, each)] = value.astype(jnp.bfloat16).reshape(each, count, width)
            return 0

        lax.fori_loop(0, chunks // each, block, 0, unroll=True)


def spread_kernel(dim, at_ref, *refs):
    *pieces, kept_ref, moved_ref, out_ref, table = refs
    step = pl.program_id(0)

    @pl.when(step == 0)
    def _():
        for n, piece in enumerate(pieces):
            db, dc, dy = n // 4, (n // 2) % 2, n % 2
            b = lax.rem(at_ref[1] + db, 2)
            c = lax.rem(at_ref[2] + dc, 2)
            y = lax.rem(at_ref[3] + dy, 2)
            table[4 * b + 2 * c + y] = piece[...]
        out_ref[...] = kept_ref[...].astype(jnp.float32) + moved_ref[...].astype(jnp.float32)

    for w in range(3):

        @pl.when(step == w + 1)
        def _(w=w):
            heads = []
            for h in range(HEADS):
                c, k, b, y = h // 8, (h // 4) % 2, (h // 2) % 2, h % 2
                low = (w * KEPT + k) * dim
                heads.append(table[4 * b + 2 * c + y, :, low : low + dim].astype(jnp.float32))
            out_ref[...] = jnp.concatenate(heads, axis=1)


def local(pix, rep, tokens, out_grad, query_weight, key_weight, value_weight, output_weight):
    grid = Grid(pix, rep)
    lines = grid.lines
    width = tokens.shape[-1]
    dim = width // HEADS
    wide = KEPT * dim
    shard = query_weight.shape[0]
    scale = 1.0 / dim**0.5
    place, rank = lax.axis_index("pix"), lax.axis_index("rep")
    a, b, c, y = place // 4, (place // 2) % 2, place % 2, rank % 2
    at = jnp.stack([a, b, c, y]).astype(jnp.int32)
    rows = tokens.reshape(-1, width)
    drows = out_grad.reshape(-1, width)
    count = rows.shape[0]
    total = 8 * count

    def gather_rows(own):
        ways = ((1, 0), (0, 1), (1, 1))
        chips = jnp.stack([own] + [grid.flip(own, db, 0, dy) for db, dy in ways])
        return chips, grid.flip(chips, 0, 1, 0)

    pieces = pl.pallas_call(
        functools.partial(pack_kernel, dim),
        compiler_params=room(8),
        out_shape=(shape_of(shard, 3 * wide),) * 4,
        in_specs=[SMEM] + [pl.BlockSpec(memory_space=pltpu.HBM)] * 3,
        out_specs=(VMEM,) * 4,
        scratch_shapes=[pltpu.VMEM((shard, width), jnp.bfloat16)] * 3
        + [pltpu.SemaphoreType.DMA((3,))],
    )(at, *[pltpu.with_memory_space_constraint(v, pltpu.HBM) for v in (query_weight, key_weight, value_weight)])
    pieces = [pieces[0]] + [grid.flip(pieces[n], n // 2, n % 2, 0) for n in range(1, 4)]
    plane = pl.pallas_call(
        plane_kernel,
        compiler_params=room(8),
        out_shape=shape_of(2, shard, 6 * wide),
        in_specs=[SMEM] + [VMEM] * 4,
        out_specs=VMEM,
    )(at, *pieces)
    xs, xc = gather_rows(rows)
    planes = grid.gather_lines(plane)

    one_head = shard == dim
    span = lines // 2
    if one_head:
        out_ws = [
            grid.send(
                output_weight,
                lambda a, b, c, g, y: (((a + s) % lines, b, a // span, g, y) if c == y else None),
            )
            for s in range(lines)
        ]
    else:
        everything = lax.all_gather(output_weight, "pix", axis=0, tiled=True)
        everything = everything.reshape(2, KEPT, 2, 2, dim, width)
        out_w = lax.dynamic_index_in_dim(everything, c, 0, keepdims=False)
        out_w = lax.dynamic_index_in_dim(
            out_w.reshape(KEPT, 4, dim, width), 2 * b + y, 1, keepdims=False
        ).reshape(wide, width)
        out_ws = [out_w]
    ds, dc = gather_rows(drows)

    owed = len(out_ws)
    head_rows = dim if one_head else wide
    project = pl.pallas_call(
        functools.partial(project_kernel, lines),
        compiler_params=room(16),
        out_shape=(shape_of(total, 3 * wide), shape_of(width, 3 * wide)),
        in_specs=[SMEM] + [VMEM] * (2 + len(planes)),
        out_specs=(VMEM,) * 2,
        scratch_shapes=[pltpu.VMEM((pix, shard, 3 * wide), jnp.bfloat16)],
        cost_estimate=pl.CostEstimate(
            flops=6 * total * width * wide, bytes_accessed=6 << 20, transcendentals=0
        ),
    )
    qkv, full = project(at, xs, xc, *planes)
    *grads_out, dqkv = pl.pallas_call(
        functools.partial(attention_kernel, scale, lines, owed),
        compiler_params=room(24),
        out_shape=(shape_of(head_rows, width),) * owed + (shape_of(total, 3 * wide),),
        in_specs=[SMEM] + [VMEM] * (3 + owed),
        out_specs=(VMEM,) * (owed + 1),
        scratch_shapes=[
            pltpu.VMEM((wide, width), jnp.bfloat16),
            pltpu.VMEM((total, wide), jnp.bfloat16),
            pltpu.VMEM((BLOCK, BLOCK), jnp.float32),
        ],
        cost_estimate=pl.CostEstimate(
            flops=6 * total * width * wide, bytes_accessed=6 << 20, transcendentals=total * 512
        ),
    )(at, ds, dc, qkv, *out_ws)
    weigh = pl.pallas_call(
        weight_kernel,
        compiler_params=room(20),
        out_shape=(shape_of(2, shard, 6 * wide),) * lines,
        in_specs=[SMEM] + [VMEM] * 3,
        out_specs=(VMEM,) * lines,
        scratch_shapes=[
            pltpu.VMEM((pix, shard, 3 * wide), jnp.bfloat16),
            pltpu.VMEM((width, 3 * wide), jnp.float32),
        ],
        cost_estimate=pl.CostEstimate(
            flops=6 * total * width * wide, bytes_accessed=5 << 20, transcendentals=0
        ),
    )
    grads_in = weigh(at, xs, xc, dqkv)

    parts = [grads_in[0]] + [grid.shift(grads_in[s], s) for s in range(1, lines)]
    if one_head:
        heads = [
            grid.send(
                grads_out[s],
                lambda a, b, c, g, y: (
                    ((a + s) % lines, b, y, g, y) if ((a + s) % lines) // span == c else None
                ),
            )
            for s in range(lines)
        ]
    else:
        whole = jnp.zeros((2, KEPT, 2, 2, dim, width), jnp.float32)
        whole = lax.dynamic_update_slice(
            whole,
            grads_out[0].astype(jnp.float32).reshape(1, KEPT, 1, 1, dim, width),
            (c, 0, b, y, 0, 0),
        ).reshape(width, width)
        heads = [lax.psum_scatter(whole, "pix", scatter_dimension=0, tiled=True)]
    kept = sum(head.astype(jnp.float32) for head in heads).astype(jnp.bfloat16)
    if one_head:
        moved = grid.send(kept, lambda a, b, c, g, y: (a, b, c, g, y ^ 1) if c == y else None)
    else:
        moved = grid.flip(kept, 0, 0, 1)
    summed = pl.pallas_call(
        sum_kernel,
        compiler_params=room(8),
        out_shape=(shape_of(shard, 3 * wide),) * 4,
        in_specs=[SMEM] + [VMEM] * len(parts),
        out_specs=(VMEM,) * 4,
    )(at, *parts)
    square = []
    for n in range(8):
        block = summed[n // 2]
        square.append(grid.flip(block, n // 4, (n // 2) % 2, n % 2) if n else block)

    input_call = pl.pallas_call(
        input_kernel,
        compiler_params=room(20),
        out_shape=(shape_of(4, count, width),) * 2,
        in_specs=[VMEM] * 2,
        out_specs=(VMEM,) * 2,
        cost_estimate=pl.CostEstimate(
            flops=6 * total * width * wide, bytes_accessed=8 << 20, transcendentals=0
        ),
    )
    own_part, other_part = input_call(dqkv, full)
    swapped = grid.flip(other_part, 0, 1, 0)
    pair = lambda i: own_part[i].astype(jnp.float32) + swapped[i].astype(jnp.float32)
    moves = [
        grid.flip(pair(i + 1).astype(jnp.bfloat16), db, 0, dy)
        for i, (db, dy) in enumerate(((1, 0), (0, 1), (1, 1)))
    ]
    dinput = pair(0) + sum(move.astype(jnp.float32) for move in moves)
    dinput = dinput.astype(jnp.bfloat16)

    grads = pl.pallas_call(
        functools.partial(spread_kernel, dim),
        compiler_params=room(12),
        out_shape=shape_of(shard, 4 * width, dtype=jnp.float32),
        grid=(4,),
        in_specs=[SMEM] + [VMEM] * 10,
        out_specs=pl.BlockSpec((shard, width), lambda i: (0, (i + 3) % 4)),
        scratch_shapes=[pltpu.VMEM((8, shard, 3 * wide), jnp.bfloat16)],
    )(at, *square, kept, moved)
    if grid.groups > 1:
        same = [[2 * g + y for g in range(grid.groups)] for y in range(2)]
        grads = lax.psum(grads, "rep", axis_index_groups=same)
    return dinput.reshape(tokens.shape), grads


def solution(mesh):
    pix, rep = mesh.shape["pix"], mesh.shape["rep"]
    sites = P(BOTH, None, None)
    rows = P("pix", None)

    def step(*operands):
        return local(pix, rep, *operands)

    return jax.shard_map(
        step,
        mesh=mesh,
        in_specs=(sites, sites, rows, rows, rows, rows),
        out_specs=(sites, rows),
        check_vma=False,
    )
```
